768 devices in a mesh: frame: 48 (over x, z_lo, core), space: 16 (over z_hi, y).
Axes of the slice: x: 4, y: 8, z: 12 (z_hi: 2, z_lo: 6; z = z_hi * 6 + z_lo), core: 2. Of those that a mesh axis runs over, the one named last changes fastest.
Arguments:
- residual_in: bfloat16 [96, 1536, 1152], P('frame', 'space'), may hold values from -40 to 40
- q_spatial: bfloat16 [96, 1536, 1152], P('frame', 'space'), may hold values from -400 to 400
- k_spatial: bfloat16 [96, 1536, 1152], P('frame', 'space'), may hold values from -12 to 12
- v_spatial: bfloat16 [96, 1536, 1152], P('frame', 'space'), may hold values from -24 to 24
- w_out: bfloat16 [1152, 1152], replicated, may hold values from -0.1875 to 0.1875
- modulation: float32 [3, 1152], replicated, may hold values from -3 to 3
- w_temporal: bfloat16 [1152, 1728], replicated, may hold values from -4 to 4
Outputs:
- residual_out: bfloat16 [96, 1536, 1152], P('frame', 'space')
- temporal_mix: bfloat16 [96, 1536, 576], P('frame', 'space')
The draws below stay inside these ranges and needn't reach their ends.
All inputs are finite; a program needn't handle non-finite values.
Results may differ from the reference program's by a relative error of at most 0.0085.
Values may be sent and summed in bfloat16 or wider, within the bound.
A program may use at most 32 MiB of HBM per device.

```python
import math
import jax
import jax.numpy as jnp
from jax import lax

D = 1152
HEADS = 16
T_HEADS = 8
TD = 576
FRAMES = 96
POSITIONS = 1536


def spatial_pair(key):
    shape = (FRAMES, POSITIONS, D)
    keys_drawn = jnp.clip(jax.random.normal(jax.random.fold_in(key, 11), shape, jnp.float32) * 1.5, -12.0, 12.0)
    queries_drawn = jax.random.normal(jax.random.fold_in(key, 12), shape, jnp.float32) * 1.5
    return (jnp.clip(queries_drawn, -400.0, 400.0), keys_drawn)


def draw_q_spatial(key, part):
    return spatial_pair(key)[0].astype(jnp.bfloat16)


def draw_k_spatial(key, part):
    return spatial_pair(key)[1].astype(jnp.bfloat16)


def draw_residual_in(key, part):
    own = jax.random.normal(jax.random.fold_in(key, 21), (FRAMES, POSITIONS, D), jnp.float32)
    values_drawn = own
    return jnp.clip(values_drawn, -40.0, 40.0).astype(jnp.bfloat16)


def draw_w_temporal(key, part):
    base = jax.random.normal(jax.random.fold_in(key, 31), (D, 3 * TD), jnp.float32) / jnp.sqrt(1.0 * D)
    return jnp.clip(base, -4.0, 4.0).astype(jnp.bfloat16)


def block_levels(key, dims, cuts, low, high):
    factor_of, own = 1.0, jax.random.fold_in(key, 6)
    for dim, shards_of in cuts:
        heights = jnp.exp(jax.random.uniform(jax.random.fold_in(own, dim), (shards_of,), jnp.float32, low / len(cuts), high / len(cuts)))
        factor_of = factor_of * jnp.repeat(heights, dims[dim] // shards_of).reshape([-1 if axis == dim else 1 for axis in range(len(dims))])
    return factor_of


def centred(key, dims, scale, bound, cuts=(), dtype=jnp.bfloat16):
    result = jax.random.normal(key, dims, jnp.float32) * scale
    if len(cuts) > 0:
        result = block_levels(key, dims, cuts, -0.22, 0.18) * result
    return jnp.clip(result, min=-bound, max=bound).astype(dtype)


def setup_inputs(seed: int = 0) -> dict:
    key_list = jax.random.split(jax.random.key(seed), 8)
    residual_in = draw_residual_in(jax.random.fold_in(key_list[7], 71), 0)
    q_spatial = draw_q_spatial(jax.random.fold_in(key_list[7], 71), 0)
    k_spatial = draw_k_spatial(jax.random.fold_in(key_list[7], 71), 0)
    v_spatial = centred(key_list[3], (FRAMES, POSITIONS, D), 4.0, 24.0, ((0, 48), (1, 16)))
    w_out = centred(key_list[4], (D, D), D ** -0.5, 0.1875)
    modulation = centred(key_list[5], (3, D), 0.7, 3.0, (), jnp.float32)
    w_temporal = draw_w_temporal(jax.random.fold_in(key_list[7], 71), 0)
    return {"residual_in": residual_in, "q_spatial": q_spatial, "k_spatial": k_spatial, "v_spatial": v_spatial, "w_out": w_out, "modulation": modulation, "w_temporal": w_temporal}


def attend_full(queries, keys_in, values_in, head_count):
    lengths = queries.shape[0]
    columns = queries.shape[1]
    head_size = columns // head_count
    query_heads = queries.astype(jnp.float32).reshape(lengths, head_count, head_size)
    key_heads = keys_in.astype(jnp.float32).reshape(keys_in.shape[0], head_count, head_size)
    value_heads = values_in.astype(jnp.float32).reshape(values_in.shape[0], head_count, head_size)
    scores = jnp.einsum('qha,kha->hqk', query_heads, key_heads) / math.sqrt(head_size)
    largest = lax.optimization_barrier(jnp.max(scores, axis=-1, keepdims=True))
    expons = jnp.exp(scores - largest)
    totals = lax.optimization_barrier(jnp.sum(expons, axis=-1, keepdims=True))
    rounded = lax.optimization_barrier(expons.astype(jnp.bfloat16)).astype(jnp.float32)
    mixed = jnp.einsum('hqk,kha->hqa', rounded, value_heads) / totals
    return jnp.transpose(mixed, (1, 0, 2)).reshape(lengths, columns).astype(jnp.bfloat16)

def temporal_full(row_block, head_count):
    frame_count, place_count, triple_width = row_block.shape
    inner = triple_width // 3
    head_size = inner // head_count
    shaped = row_block.astype(jnp.float32).reshape(frame_count, place_count, 3, head_count, head_size)
    queries = shaped[:, :, 0]
    keys_in = shaped[:, :, 1]
    values_in = shaped[:, :, 2]
    scores = jnp.einsum('fpha,gpha->phfg', queries, keys_in) / math.sqrt(head_size)
    largest = lax.optimization_barrier(jnp.max(scores, axis=-1, keepdims=True))
    expons = jnp.exp(scores - largest)
    totals = lax.optimization_barrier(jnp.sum(expons, axis=-1, keepdims=True))
    rounded = lax.optimization_barrier(expons.astype(jnp.bfloat16)).astype(jnp.float32)
    mixed = jnp.einsum('phfg,gpha->phfa', rounded, values_in) / totals
    return jnp.transpose(mixed, (2, 0, 1, 3)).reshape(frame_count, place_count, inner).astype(jnp.bfloat16)

def modulate(residual_out, modulation):
    values32 = residual_out.astype(jnp.float32)
    center = lax.optimization_barrier(jnp.mean(values32, axis=-1, keepdims=True))
    spread = lax.optimization_barrier(jnp.mean((values32 - center) ** 2, axis=-1, keepdims=True))
    normed = (values32 - center) * lax.rsqrt(spread + 1e-06) * (1.0 + modulation[1]) + modulation[0]
    return normed.astype(jnp.bfloat16)

def reference(residual_in, q_spatial, k_spatial, v_spatial, w_out, modulation, w_temporal):
    spatial_mix = lax.map(lambda triple: attend_full(triple[0], triple[1], triple[2], HEADS), (q_spatial, k_spatial, v_spatial))
    branch = jnp.dot(spatial_mix.reshape(-1, D), w_out, preferred_element_type=jnp.float32).reshape(residual_in.shape)
    residual_out = (residual_in.astype(jnp.float32) + modulation[2] * branch).astype(jnp.bfloat16)
    normed = modulate(residual_out, modulation)
    projected = jnp.dot(normed.reshape(-1, D), w_temporal, preferred_element_type=jnp.float32).astype(jnp.bfloat16)
    projected = projected.reshape(FRAMES, POSITIONS, 3 * TD)
    block = math.gcd(POSITIONS, 128)
    blocks = projected.reshape(FRAMES, POSITIONS // block, block, 3 * TD).transpose(1, 0, 2, 3)
    temporal = lax.map(lambda row_block: temporal_full(row_block, T_HEADS), blocks)
    temporal_mix = temporal.transpose(1, 0, 2, 3).reshape(FRAMES, POSITIONS, TD)
    return (residual_out, temporal_mix)
```

```python
import functools
import math

import jax
import jax.numpy as jnp
from jax import lax
from jax.experimental import pallas as pl
from jax.experimental.pallas import tpu as pltpu
from jax.sharding import PartitionSpec as P

MESH = pl.DeviceIdType.MESH
HEAD = 72
T_HEADS = 8
BF = jnp.bfloat16
F32 = jnp.float32
EXP2_SCALE = math.log2(math.e) / math.sqrt(HEAD)


def lane_iota(rows):
    return lax.broadcasted_iota(jnp.int32, (rows, 128), 1)


def roll_lanes(x, shift):
    shift = shift % 128
    if shift == 0:
        return x
    return pltpu.roll(x, shift, axis=1)


def send(src, dst, ssem, rsem, device):
    return pltpu.make_async_remote_copy(
        src_ref=src, dst_ref=dst, send_sem=ssem, recv_sem=rsem, device_id=device, device_id_type=MESH
    )


def spatial_kernel(
    q_ref, k_ref, v_ref, out_ref,
    sbk, sbq, sbv, zrk, zrq, zrv, fk, fq, fv, qs, k0, k1, vs, pr, ob, zro,
    zs, zr, ys, yr, zos, zor, yos, yor,
):
    f = lax.axis_index("frame")
    s = lax.axis_index("space")
    a = s // 8
    y = lax.rem(s, 8)
    far = 1 - a
    partner = (f, far * 8 + y)
    places = q_ref.shape[1]
    half = places // 2

    barrier = pltpu.get_barrier_semaphore()
    pl.semaphore_signal(barrier, inc=1, device_id=partner, device_id_type=MESH)

    def greet(j, carry):
        pl.semaphore_signal(
            barrier, inc=1, device_id=(f, a * 8 + lax.rem(y + j, 8)), device_id_type=MESH
        )
        return carry

    lax.fori_loop(1, 8, greet, 0)

    lanes = lane_iota(places)
    half_lanes = lane_iota(half)

    def tile(ref, fr, index):
        return ref[fr, :, 128 * index : 128 * index + 128].astype(F32)

    def main_of(ref, fr, pair):
        low = tile(ref, fr, pair)
        if pair == 0:
            return low.astype(BF)
        high = tile(ref, fr, pair + 1)
        return roll_lanes(jnp.where(lanes >= 16 * pair, low, high), -16 * pair).astype(BF)

    def pack_k(fr):
        for pair in range(8):
            sbk[fr, pair, 0:places] = main_of(k_ref, fr, pair)
            left = jnp.where(
                lanes < 16,
                roll_lanes(tile(k_ref, fr, pair + 1), -16 * pair),
                jnp.where(
                    lanes < 32,
                    roll_lanes(tile(q_ref, fr, pair + 1), 16 - 16 * pair),
                    roll_lanes(tile(v_ref, fr, pair + 1), 32 - 16 * pair),
                ),
            )
            joined = jnp.where(half_lanes < 64, left[0:half], roll_lanes(left[half:places], 64))
            sbk[fr, pair, places : places + half] = joined.astype(BF)

    def pack(ref, buf, fr):
        for pair in range(8):
            buf[fr, pair] = main_of(ref, fr, pair)

    sent = ((sbk, zrk, fk), (sbq, zrq, fq), (sbv, zrv, fv))

    def z_copy(t, j):
        buf, relay, final = sent[t]
        target = lax.rem(y + j, 8)
        return send(buf.at[far, target], relay.at[j], zs.at[t, j], zr.at[t, j], partner)

    def z_home(t):
        buf, relay, final = sent[t]
        return send(buf.at[far, y], final.at[s], zs.at[t, 0], zr.at[t, 0], partner)

    def y_copy(t, j):
        buf, relay, final = sent[t]
        target = lax.rem(y + j, 8)
        return send(
            buf.at[a, target], final.at[s], ys.at[0, t, j], yr.at[0, t, j], (f, a * 8 + target)
        )

    def y_relay(t, j):
        buf, relay, final = sent[t]
        target = lax.rem(y + j, 8)
        return send(
            relay.at[j], final.at[far * 8 + y], ys.at[1, t, j], yr.at[1, t, j],
            (f, a * 8 + target),
        )

    def each(low, high, body):
        def step(j, carry):
            body(j)
            return carry

        lax.fori_loop(low, high, step, 0)

    pack_k(far)
    pl.semaphore_wait(barrier, 8)

    def z_start(t):
        each(1, 8, lambda j: z_copy(t, j).start())
        z_home(t).start()

    def y_start(t):
        each(1, 8, lambda j: y_copy(t, j).start())

    z_start(0)
    pack(q_ref, sbq, far)
    z_start(1)
    pack(v_ref, sbv, far)
    z_start(2)
    pack_k(a)
    y_start(0)
    pack(q_ref, sbq, a)
    y_start(1)
    pack(v_ref, sbv, a)
    y_start(2)
    fk[s] = sbk[a, y]
    fq[s] = sbq[a, y]
    fv[s] = sbv[a, y]

    def forward(t, j):
        z_copy(t, j).wait_recv()
        y_relay(t, j).start()

    def settle(t):
        z_home(t).wait_recv()
        each(1, 8, lambda j: y_copy(t, j).wait_recv())
        each(1, 8, lambda j: y_relay(t, j).wait_recv())

    each(1, 8, lambda j: forward(0, j))
    each(1, 8, lambda j: forward(1, j))
    settle(0)
    settle(1)

    zero = jnp.zeros((places, 128), F32)

    def spread(block):
        rows = pl.ds(pl.multiple_of(block * places, places), places)
        main = fk[block, 0:places].astype(F32)
        packed = fk[block, places : places + half].astype(F32)
        left = jnp.concatenate([packed, roll_lanes(packed, 64)], axis=0)
        k0[rows, :] = jnp.where(lanes < HEAD, main, zero).astype(BF)
        k1[rows, 0:128] = jnp.where(lanes < HEAD, zero, main).astype(BF)
        k1[rows, 128:256] = jnp.where(lanes < 16, left, zero).astype(BF)
        qs[rows, 0:128] = fq[block]
        qs[rows, 128:256] = roll_lanes(left, -16).astype(BF)
        vs[rows, 128:256] = jnp.where(
            lanes < 16, roll_lanes(left, -32), jnp.where(lanes == 16, 1.0, 0.0)
        ).astype(BF)

    each(0, 16, spread)

    big = 4 * places

    def weigh(step):
        rows = pl.ds(pl.multiple_of(step * big, big), big)
        for head in range(2):
            if head == 0:
                left_side, keys = qs[rows, 0:128], k0[...]
            else:
                left_side, keys = qs[rows, :], k1[...]
            scores = lax.dot_general(
                left_side, keys, (((1,), (1,)), ((), ())), preferred_element_type=F32
            )
            largest = jnp.max(scores, axis=1, keepdims=True)
            pr[head, rows, :] = jnp.exp2((scores - largest) * EXP2_SCALE).astype(BF)
        forward(2, 2 * step + 1)

        @pl.when(step < 3)
        def _():
            forward(2, 2 * step + 2)

    each(0, 4, weigh)
    settle(2)

    def place_v(block):
        rows = pl.ds(pl.multiple_of(block * places, places), places)
        vs[rows, 0:128] = fv[block]

    each(0, 16, place_v)

    sub_lanes = lane_iota(16)

    def mix(first):
        rows = pl.ds(pl.multiple_of(first * places, places), big)
        mixed = []
        for head in range(2):
            product = jnp.dot(pr[head, rows, :], vs[...], preferred_element_type=F32)
            inverse = 1.0 / product[:, 144:145]
            mixed.append(product * inverse)
        for part in range(4):
            cut = slice(part * places, (part + 1) * places)
            ob[first + part, 0:places] = jnp.where(
                lanes < HEAD, mixed[0][cut, 0:128], mixed[1][cut, 0:128]
            ).astype(BF)
            rest = mixed[1][cut, 128:256]
            packed = rest[0:16]
            for group in range(1, 6):
                moved = roll_lanes(rest[16 * group : 16 * group + 16], 16 * group)
                packed = jnp.where(sub_lanes < 16 * group, packed, moved)
            ob[first + part, places : places + 16] = packed.astype(BF)

    def z_back(target):
        return send(
            ob.at[far * 8 + target], zro.at[target], zos.at[target], zor.at[target], partner
        )

    def z_back_home():
        return send(ob.at[far * 8 + y], out_ref.at[a, y], zos.at[y], zor.at[y], partner)

    def y_back(j):
        target = lax.rem(y + j, 8)
        return send(
            ob.at[a * 8 + target], out_ref.at[a, y], yos.at[0, j], yor.at[0, j],
            (f, a * 8 + target),
        )

    def y_back_relay(target):
        j = lax.rem(target + 8 - y, 8)
        return send(
            zro.at[target], out_ref.at[far, y], yos.at[1, j], yor.at[1, j], (f, a * 8 + target)
        )

    def z_back_start(target):
        @pl.when(target != y)
        def _():
            z_back(target).start()

        @pl.when(target == y)
        def _():
            z_back_home().start()

    def far_part(step):
        mix(far * 8 + 4 * step)
        each(4 * step, 4 * step + 4, z_back_start)

    def near_part(step):
        mix(a * 8 + 4 * step)

    each(0, 2, far_part)
    each(0, 2, near_part)
    each(1, 8, lambda j: y_back(j).start())
    out_ref[a, y] = ob[s]

    def relay_back(target):
        @pl.when(target != y)
        def _():
            z_back(target).wait_recv()
            y_back_relay(target).start()

    each(0, 8, relay_back)
    z_back_home().wait_recv()
    each(1, 8, lambda j: y_back(j).wait_recv())

    def relay_end(j):
        copy = send(
            zro.at[0], out_ref.at[far, 0], yos.at[1, j], yor.at[1, j], (f, a * 8 + lax.rem(y + j, 8))
        )
        copy.wait_recv()
        copy.wait_send()

    each(1, 8, relay_end)
    each(1, 8, lambda j: y_back(j).wait_send())

    each(0, 8, lambda target: z_back(target).wait_send())
    for t in range(3):
        z_home(t).wait_send()
        each(1, 8, lambda j: z_copy(t, j).wait_send())
        each(1, 8, lambda j: y_copy(t, j).wait_send())
        each(1, 8, lambda j: y_relay(t, j).wait_send())


def one_hot(rows_of):
    size = 192
    row = lax.broadcasted_iota(jnp.int32, (size, size), 0)
    column = lax.broadcasted_iota(jnp.int32, (size, size), 1)
    return jnp.where(column == rows_of(row), 1.0, 0.0).astype(BF)


def temporal_kernel(
    mix_ref, res_ref, wo_ref, mod_ref, wt_ref, res_out, mix_out,
    am, wp, pf, sbf, rbf, tm, sb2, rb2, fs, fr_sem, gs, gr,
):
    f = lax.axis_index("frame")
    s = lax.axis_index("space")
    n = lax.axis_size("frame")
    barrier = pltpu.get_barrier_semaphore()

    def each(low, high, body):
        def step(j, carry):
            body(j)
            return carry

        lax.fori_loop(low, high, step, 0)

    each(
        1, n,
        lambda i: pl.semaphore_signal(
            barrier, inc=1, device_id=(lax.rem(f + i, n), s), device_id_type=MESH
        ),
    )

    places = res_ref.shape[1]
    width = wt_ref.shape[1]
    inner = width // 3
    lanes16 = lane_iota(16)
    for pair in range(8):
        wp[128 * pair : 128 * pair + 128] = wo_ref[144 * pair : 144 * pair + 128]
        wp[1024 + 16 * pair : 1040 + 16 * pair] = wo_ref[144 * pair + 128 : 144 * pair + 144]
    for frame in range(2):
        base = frame * places
        for pair in range(8):
            am[base : base + places, 128 * pair : 128 * pair + 128] = mix_ref[frame, pair, 0:places]
        packs = [mix_ref[frame, pair, places : places + 16].astype(F32) for pair in range(8)]
        for group in range(6):
            joined = roll_lanes(packs[0], -16 * group)
            for pair in range(1, 8):
                moved = roll_lanes(packs[pair], 16 * pair - 16 * group)
                joined = jnp.where(lanes16 < 16 * pair, joined, moved)
            am[base + 16 * group : base + 16 * group + 16, 1024:1152] = joined.astype(BF)

    branch = jnp.dot(am[...], wp[...], preferred_element_type=F32)
    res = res_ref[...].reshape(2 * places, res_ref.shape[2]).astype(F32)
    res = (res + mod_ref[2:3, :] * branch).astype(BF)
    res_out[...] = res.reshape(res_out.shape)
    values = res.astype(F32)
    center = jnp.mean(values, axis=1, keepdims=True)
    moved = values - center
    spread = jnp.mean(moved * moved, axis=1, keepdims=True)
    normed = moved * lax.rsqrt(spread + 1e-06) * (1.0 + mod_ref[1:2, :]) + mod_ref[0:1, :]
    normed = normed.astype(BF)

    by_group = one_hot(lambda r: lax.rem(r, 2) * 96 + 2 * (r // 4) + lax.rem(r // 2, 2))
    by_place = one_hot(lambda r: 4 * (lax.rem(r, 96) // 2) + 2 * (r // 96) + lax.rem(r, 2))
    to_group = one_hot(lambda r: lax.rem(r // 2, 2) * 96 + 2 * (r // 4) + lax.rem(r, 2))
    to_rows = one_hot(lambda r: 4 * (lax.rem(r, 96) // 2) + 2 * lax.rem(r, 2) + r // 96)

    grouped = jnp.dot(by_group, normed, preferred_element_type=F32).astype(BF)
    pf[:, 1664:1792] = jnp.zeros((2 * places, 128), F32)
    pf[:, 0:width] = jnp.dot(grouped, wt_ref[...], preferred_element_type=F32)

    def eight(g):
        return pl.ds(pl.multiple_of(8 * g, 8), 8)

    def cut(g):
        both = pf[eight(g), :]
        sbf[2 * g] = both[0:4].astype(BF)
        sbf[2 * g + 1] = both[4:8].astype(BF)

    each(0, n // 2, cut)
    pl.semaphore_wait(barrier, n - 1)

    def forth(i):
        target = lax.rem(f + i, n)
        return send(sbf.at[target], rbf.at[f], fs.at[i], fr_sem.at[i], (target, s))

    each(1, n, lambda i: forth(i).start())
    rbf[f] = sbf[f]
    each(1, n, lambda i: forth(i).wait_recv())

    def gather(g):
        pf[eight(g), :] = jnp.concatenate(
            [rbf[2 * g].astype(F32), rbf[2 * g + 1].astype(F32)], axis=0
        )

    each(0, n // 2, gather)
    rows = jnp.dot(by_place, pf[...].astype(BF), preferred_element_type=F32).astype(BF)
    lanes256 = lax.broadcasted_iota(jnp.int32, (96, 256), 1)
    tm[...] = jnp.zeros(tm.shape, F32)
    for p in range(2):
        block = rows[p * 96 : p * 96 + 96]
        for head in range(T_HEADS):
            start = head * HEAD
            queries = block[:, start : start + HEAD]
            keys = block[:, inner + start : inner + start + HEAD]
            window = (start // 128) * 128
            window = min(window, 384)
            scores = lax.dot_general(
                queries, keys, (((1,), (1,)), ((), ())), preferred_element_type=F32
            )
            largest = jnp.max(scores, axis=1, keepdims=True)
            expons = jnp.exp2((scores - largest) * EXP2_SCALE)
            totals = jnp.sum(expons, axis=1, keepdims=True)
            vals = block[:, 2 * inner + window : min(2 * inner + window + 256, 1792)]
            product = jnp.dot(expons.astype(BF), vals, preferred_element_type=F32) / totals
            near = lanes256[:, : vals.shape[1]] + window
            held = (near >= start) & (near < start + HEAD)
            spot = (slice(p * 96, p * 96 + 96), slice(window, window + vals.shape[1]))
            tm[spot] = jnp.where(held, product, tm[spot])

    back = jnp.dot(to_group, tm[...].astype(BF), preferred_element_type=F32)
    pf[:, 0:640] = back

    def cut_back(g):
        both = pf[eight(g), 0:640]
        sb2[2 * g] = both[0:4].astype(BF)
        sb2[2 * g + 1] = both[4:8].astype(BF)

    each(0, n // 2, cut_back)

    def home(i):
        target = lax.rem(f + i, n)
        return send(sb2.at[target], rb2.at[f], gs.at[i], gr.at[i], (target, s))

    each(1, n, lambda i: home(i).start())
    rb2[f] = sb2[f]
    each(1, n, lambda i: home(i).wait_recv())

    def gather_back(g):
        pf[eight(g), 0:640] = jnp.concatenate(
            [rb2[2 * g].astype(F32), rb2[2 * g + 1].astype(F32)], axis=0
        )

    each(0, n // 2, gather_back)
    final = jnp.dot(to_rows, pf[:, 0:640].astype(BF), preferred_element_type=F32)
    mix_out[...] = final[:, 0:inner].astype(BF).reshape(mix_out.shape)
    each(1, n, lambda i: forth(i).wait_send())
    each(1, n, lambda i: home(i).wait_send())


def per_device(residual_in, q_spatial, k_spatial, v_spatial, w_out, modulation, w_temporal):
    frames, places, features = residual_in.shape
    half = places // 2
    total = 16 * places
    vmem = pl.BlockSpec(memory_space=pltpu.VMEM)
    dma = pltpu.SemaphoreType.DMA
    mixed = pl.pallas_call(
        spatial_kernel,
        out_shape=jax.ShapeDtypeStruct((2, 8, places + 16, 128), BF),
        in_specs=[vmem] * 3,
        out_specs=vmem,
        scratch_shapes=[
            pltpu.VMEM((2, 8, places + half, 128), BF),
            pltpu.VMEM((2, 8, places, 128), BF),
            pltpu.VMEM((2, 8, places, 128), BF),
            pltpu.VMEM((8, places + half, 128), BF),
            pltpu.VMEM((8, places, 128), BF),
            pltpu.VMEM((8, places, 128), BF),
            pltpu.VMEM((16, places + half, 128), BF),
            pltpu.VMEM((16, places, 128), BF),
            pltpu.VMEM((16, places, 128), BF),
            pltpu.VMEM((total, 256), BF),
            pltpu.VMEM((total, 128), BF),
            pltpu.VMEM((total, 256), BF),
            pltpu.VMEM((total, 256), BF),
            pltpu.VMEM((2, total, total), BF),
            pltpu.VMEM((16, places + 16, 128), BF),
            pltpu.VMEM((8, places + 16, 128), BF),
            dma((3, 8)), dma((3, 8)), dma((2, 3, 8)), dma((2, 3, 8)),
            dma((8,)), dma((8,)), dma((2, 8)), dma((2, 8)),
        ],
        compiler_params=pltpu.CompilerParams(
            collective_id=1, has_side_effects=True, vmem_limit_bytes=40 << 20
        ),
        name="spatial_attention",
    )(q_spatial, k_spatial, v_spatial)
    width = w_temporal.shape[1]
    return pl.pallas_call(
        temporal_kernel,
        out_shape=(
            jax.ShapeDtypeStruct((frames, places, features), BF),
            jax.ShapeDtypeStruct((frames, places, width // 3), BF),
        ),
        in_specs=[vmem] * 5,
        out_specs=(vmem, vmem),
        scratch_shapes=[
            pltpu.VMEM((2 * places, features), BF),
            pltpu.VMEM((features, features), BF),
            pltpu.VMEM((2 * places, 1792), F32),
            pltpu.VMEM((48, 4, 1792), BF),
            pltpu.VMEM((48, 4, 1792), BF),
            pltpu.VMEM((2 * places, 640), F32),
            pltpu.VMEM((48, 4, 640), BF),
            pltpu.VMEM((48, 4, 640), BF),
            dma((48,)), dma((48,)), dma((48,)), dma((48,)),
        ],
        compiler_params=pltpu.CompilerParams(
            collective_id=2, has_side_effects=True, vmem_limit_bytes=40 << 20
        ),
        name="temporal_attention",
    )(mixed, residual_in, w_out, modulation, w_temporal)


def solution(mesh):
    return jax.shard_map(
        per_device,
        mesh=mesh,
        in_specs=(
            P("frame", "space", None),
            P("frame", "space", None),
            P("frame", "space", None),
            P("frame", "space", None),
            P(),
            P(),
            P(),
        ),
        out_specs=(P("frame", "space", None), P("frame", "space", None)),
        check_vma=False,
    )
```

```python
import functools
import math

import jax
import jax.numpy as jnp
from jax import lax
from jax.experimental import pallas as pl
from jax.experimental.pallas import tpu as pltpu
from jax.sharding import PartitionSpec as P

MESH = pl.DeviceIdType.MESH
HEAD = 72
T_HEADS = 8
BF = jnp.bfloat16
F32 = jnp.float32
ORDER = (3, 2, 4, 1, 5)
EXP2_SCALE = math.log2(math.e) / math.sqrt(HEAD)


def lane_iota(rows):
    return lax.broadcasted_iota(jnp.int32, (rows, 128), 1)


def roll_lanes(x, shift):
    shift = shift % 128
    if shift == 0:
        return x
    return pltpu.roll(x, shift, axis=1)


def send(src, dst, ssem, rsem, device):
    return pltpu.make_async_remote_copy(
        src_ref=src, dst_ref=dst, send_sem=ssem, recv_sem=rsem, device_id=device, device_id_type=MESH
    )


def one_hot(rows_of):
    size = 192
    row = lax.broadcasted_iota(jnp.int32, (size, size), 0)
    column = lax.broadcasted_iota(jnp.int32, (size, size), 1)
    return jnp.where(column == rows_of(row), 1.0, 0.0).astype(BF)


def block_kernel(
    res_hbm, q_hbm, k_hbm, v_hbm, wo_hbm, mod_ref, wt_hbm, res_out, mix_out,
    q_ref, k_ref, v_ref, res_ref, wp, wt,
    sbk, sbq, sbv, zrk, zrq, zrv, fk, fq, fv, qs, k0, k1, vs, pr, ob, zro, mixb,
    am, pf, sb, zx, rb, tm, sb2, zx2, rb2,
    ld, zs, zr, ys, yr, zos, zor, yos, yor, ts, tr, xs, xr, us, ur, ws, wr,
):
    f = lax.axis_index("frame")
    s = lax.axis_index("space")
    a = s // 8
    y = lax.rem(s, 8)
    far = 1 - a
    partner = (f, far * 8 + y)
    places = q_ref.shape[1]
    core = lax.rem(f, 2)
    z = lax.rem(f // 2, 6)
    kme = (f // 12) * 2 + core

    def peer(k, level):
        return (((k // 2) * 6 + level) * 2 + lax.rem(k, 2), s)

    loads = [
        pltpu.make_async_copy(k_hbm, k_ref, ld.at[0]),
        pltpu.make_async_copy(q_hbm, q_ref, ld.at[1]),
        pltpu.make_async_copy(v_hbm, v_ref, ld.at[2]),
        pltpu.make_async_copy(res_hbm, res_ref, ld.at[3]),
        pltpu.make_async_copy(wt_hbm, wt, ld.at[4]),
    ]
    for pair in range(8):
        loads.append(
            pltpu.make_async_copy(
                wo_hbm.at[pl.ds(144 * pair, 128)], wp.at[pl.ds(128 * pair, 128)], ld.at[5 + 2 * pair]
            )
        )
        loads.append(
            pltpu.make_async_copy(
                wo_hbm.at[pl.ds(144 * pair + 128, 16)],
                wp.at[pl.ds(1024 + 16 * pair, 16)],
                ld.at[6 + 2 * pair],
            )
        )
    for load in loads[:3]:
        load.start()
    half = places // 2

    barrier = pltpu.get_barrier_semaphore()
    pl.semaphore_signal(barrier, inc=1, device_id=partner, device_id_type=MESH)

    def greet(j, carry):
        pl.semaphore_signal(
            barrier, inc=1, device_id=(f, a * 8 + lax.rem(y + j, 8)), device_id_type=MESH
        )
        return carry

    lax.fori_loop(1, 8, greet, 0)

    def greet_level(j, carry):
        pl.semaphore_signal(
            barrier, inc=1, device_id=peer(kme, lax.rem(z + j, 6)), device_id_type=MESH
        )
        return carry

    lax.fori_loop(1, 6, greet_level, 0)

    def greet_row(j, carry):
        pl.semaphore_signal(
            barrier, inc=1, device_id=peer(lax.rem(kme + j, 8), z), device_id_type=MESH
        )
        return carry

    lax.fori_loop(1, 8, greet_row, 0)
    for load in loads[:3]:
        load.wait()
    for load in loads[3:]:
        load.start()

    lanes = lane_iota(places)
    half_lanes = lane_iota(half)

    def tile(ref, fr, index):
        return ref[fr, :, 128 * index : 128 * index + 128].astype(F32)

    def main_of(ref, fr, pair):
        low = tile(ref, fr, pair)
        if pair == 0:
            return low.astype(BF)
        high = tile(ref, fr, pair + 1)
        return roll_lanes(jnp.where(lanes >= 16 * pair, low, high), -16 * pair).astype(BF)

    def pack_k(fr):
        for pair in range(8):
            sbk[fr, pair, 0:places] = main_of(k_ref, fr, pair)
            left = jnp.where(
                lanes < 16,
                roll_lanes(tile(k_ref, fr, pair + 1), -16 * pair),
                jnp.where(
                    lanes < 32,
                    roll_lanes(tile(q_ref, fr, pair + 1), 16 - 16 * pair),
                    roll_lanes(tile(v_ref, fr, pair + 1), 32 - 16 * pair),
                ),
            )
            joined = jnp.where(half_lanes < 64, left[0:half], roll_lanes(left[half:places], 64))
            sbk[fr, pair, places : places + half] = joined.astype(BF)

    def pack(ref, buf, fr):
        for pair in range(8):
            buf[fr, pair] = main_of(ref, fr, pair)

    sent = ((sbk, zrk, fk), (sbq, zrq, fq), (sbv, zrv, fv))

    def z_copy(t, j):
        buf, relay, final = sent[t]
        target = lax.rem(y + j, 8)
        return send(buf.at[far, target], relay.at[j], zs.at[t, j], zr.at[t, j], partner)

    def z_home(t):
        buf, relay, final = sent[t]
        return send(buf.at[far, y], final.at[s], zs.at[t, 0], zr.at[t, 0], partner)

    def y_copy(t, j):
        buf, relay, final = sent[t]
        target = lax.rem(y + j, 8)
        return send(
            buf.at[a, target], final.at[s], ys.at[0, t, j], yr.at[0, t, j], (f, a * 8 + target)
        )

    def y_relay(t, j):
        buf, relay, final = sent[t]
        target = lax.rem(y + j, 8)
        return send(
            relay.at[j], final.at[far * 8 + y], ys.at[1, t, j], yr.at[1, t, j],
            (f, a * 8 + target),
        )

    def each(low, high, body):
        def step(j, carry):
            body(j)
            return carry

        lax.fori_loop(low, high, step, 0)

    pack_k(far)
    pl.semaphore_wait(barrier, 20)

    def z_start(t):
        each(1, 8, lambda j: z_copy(t, j).start())
        z_home(t).start()

    def y_start(t):
        each(1, 8, lambda j: y_copy(t, j).start())

    z_start(0)
    pack(q_ref, sbq, far)
    z_start(1)
    pack(v_ref, sbv, far)
    z_start(2)
    pack_k(a)
    y_start(0)
    pack(q_ref, sbq, a)
    y_start(1)
    pack(v_ref, sbv, a)
    y_start(2)
    fk[s] = sbk[a, y]
    fq[s] = sbq[a, y]
    fv[s] = sbv[a, y]

    def forward(t, j):
        z_copy(t, j).wait_recv()
        y_relay(t, j).start()

    def settle(t):
        z_home(t).wait_recv()
        each(1, 8, lambda j: y_copy(t, j).wait_recv())
        each(1, 8, lambda j: y_relay(t, j).wait_recv())

    each(1, 8, lambda j: forward(0, j))
    each(1, 8, lambda j: forward(1, j))
    settle(0)
    settle(1)

    zero = jnp.zeros((places, 128), F32)

    def spread(block):
        rows = pl.ds(pl.multiple_of(block * places, places), places)
        main = fk[block, 0:places].astype(F32)
        packed = fk[block, places : places + half].astype(F32)
        left = jnp.concatenate([packed, roll_lanes(packed, 64)], axis=0)
        k0[rows, :] = jnp.where(lanes < HEAD, main, zero).astype(BF)
        k1[rows, 0:128] = jnp.where(lanes < HEAD, zero, main).astype(BF)
        k1[rows, 128:256] = jnp.where(lanes < 16, left, zero).astype(BF)
        qs[rows, 0:128] = fq[block]
        qs[rows, 128:256] = roll_lanes(left, -16).astype(BF)
        vs[rows, 128:256] = jnp.where(
            lanes < 16, roll_lanes(left, -32), jnp.where(lanes == 16, 1.0, 0.0)
        ).astype(BF)

    each(0, 16, spread)

    big = 4 * places

    def weigh(step):
        rows = pl.ds(pl.multiple_of(step * big, big), big)
        for head in range(2):
            if head == 0:
                left_side, keys = qs[rows, 0:128], k0[...]
            else:
                left_side, keys = qs[rows, :], k1[...]
            scores = lax.dot_general(
                left_side, keys, (((1,), (1,)), ((), ())), preferred_element_type=F32
            )
            largest = jnp.max(scores, axis=1, keepdims=True)
            pr[head, rows, :] = jnp.exp2((scores - largest) * EXP2_SCALE).astype(BF)
        forward(2, 2 * step + 1)

        @pl.when(step < 3)
        def _():
            forward(2, 2 * step + 2)

    each(0, 4, weigh)
    settle(2)

    def place_v(block):
        rows = pl.ds(pl.multiple_of(block * places, places), places)
        vs[rows, 0:128] = fv[block]

    each(0, 16, place_v)

    sub_lanes = lane_iota(16)

    def mix(first):
        rows = pl.ds(pl.multiple_of(first * places, places), big)
        mixed = []
        for head in range(2):
            product = jnp.dot(pr[head, rows, :], vs[...], preferred_element_type=F32)
            inverse = 1.0 / product[:, 144:145]
            mixed.append(product * inverse)
        for part in range(4):
            cut = slice(part * places, (part + 1) * places)
            ob[first + part, 0:places] = jnp.where(
                lanes < HEAD, mixed[0][cut, 0:128], mixed[1][cut, 0:128]
            ).astype(BF)
            rest = mixed[1][cut, 128:256]
            packed = rest[0:16]
            for group in range(1, 6):
                moved = roll_lanes(rest[16 * group : 16 * group + 16], 16 * group)
                packed = jnp.where(sub_lanes < 16 * group, packed, moved)
            ob[first + part, places : places + 16] = packed.astype(BF)

    def z_back(target):
        return send(
            ob.at[far * 8 + target], zro.at[target], zos.at[target], zor.at[target], partner
        )

    def z_back_home():
        return send(ob.at[far * 8 + y], mixb.at[1, y], zos.at[y], zor.at[y], partner)

    def y_back(j):
        target = lax.rem(y + j, 8)
        return send(
            ob.at[a * 8 + target], mixb.at[0, y], yos.at[0, j], yor.at[0, j],
            (f, a * 8 + target),
        )

    def y_back_relay(target):
        j = lax.rem(target + 8 - y, 8)
        return send(
            zro.at[target], mixb.at[1, y], yos.at[1, j], yor.at[1, j], (f, a * 8 + target)
        )

    def z_back_start(target):
        @pl.when(target != y)
        def _():
            z_back(target).start()

        @pl.when(target == y)
        def _():
            z_back_home().start()

    def far_part(step):
        mix(far * 8 + 4 * step)
        each(4 * step, 4 * step + 4, z_back_start)

    def near_part(step):
        mix(a * 8 + 4 * step)

    each(0, 2, far_part)
    each(0, 2, near_part)
    each(1, 8, lambda j: y_back(j).start())
    mixb[0, y] = ob[s]

    for load in loads[3:]:
        load.wait()

    def project(kind, frame):
        packs = [mixb[kind, pair, places : places + 16].astype(F32) for pair in range(8)]
        for pair in range(8):
            am[kind, :, 128 * pair : 128 * pair + 128] = mixb[kind, pair, 0:places]
        for group in range(6):
            joined = roll_lanes(packs[0], -16 * group)
            for pair in range(1, 8):
                moved = roll_lanes(packs[pair], 16 * pair - 16 * group)
                joined = jnp.where(sub_lanes < 16 * pair, joined, moved)
            am[kind, 16 * group : 16 * group + 16, 1024:1152] = joined.astype(BF)
        branch = jnp.dot(am[kind], wp[...], preferred_element_type=F32)
        res = (res_ref[frame].astype(F32) + mod_ref[2:3, :] * branch).astype(BF)
        res_out[frame] = res
        values = res.astype(F32)
        center = jnp.mean(values, axis=1, keepdims=True)
        moved = values - center
        deviation = jnp.mean(moved * moved, axis=1, keepdims=True)
        normed = moved * lax.rsqrt(deviation + 1e-06) * (1.0 + mod_ref[1:2, :]) + mod_ref[0:1, :]
        pf[0:places, 0:width] = lax.dot_general(
            normed.astype(BF), wt[...], (((1,), (1,)), ((), ())), preferred_element_type=F32
        )

        def cut(g):
            eight = pf[pl.ds(pl.multiple_of(8 * g, 8), 8), :]
            for t in range(4):
                sb[kind, 4 * g + t] = eight[2 * t : 2 * t + 2].astype(BF)

        each(0, places // 8, cut)

    def level_copy(kind, j):
        level = lax.rem(z + j, 6)
        return send(
            sb.at[kind, pl.ds(8 * level, 8)], zx.at[kind, z], ts.at[kind, level], tr.at[kind, z],
            peer(kme, level),
        )

    def level_arrival(kind, level):
        return send(
            sb.at[kind, pl.ds(0, 8)], zx.at[kind, level], ts.at[kind, level], tr.at[kind, level],
            peer(kme, level),
        )

    def row_copy(kind, level, j, own):
        k = lax.rem(kme + j, 8)
        source = sb.at[kind, 8 * z + k] if own else zx.at[kind, level, k]
        return send(
            source, rb.at[kind, level * 8 + kme], xs.at[kind, level, k], xr.at[kind, level, kme],
            peer(k, z),
        )

    def row_arrival(kind, level, j):
        k = lax.rem(kme + j, 8)
        return send(
            sb.at[kind, 0], rb.at[kind, level * 8 + k], xs.at[kind, level, k],
            xr.at[kind, level, k], peer(k, z),
        )

    def exchange(kind):
        for j in ORDER:
            level_copy(kind, j).start()
        each(1, 8, lambda j: row_copy(kind, z, j, True).start())
        rb[kind, 8 * z + kme] = sb[kind, 8 * z + kme]

    def relay_level(kind, j):
        level = lax.rem(z + j, 6)
        level_arrival(kind, level).wait_recv()
        each(1, 8, lambda i: row_copy(kind, level, i, False).start())
        rb[kind, 8 * level + kme] = zx[kind, level, kme]

    each(1, 8, lambda j: y_back(j).wait_recv())
    width = wt.shape[0]
    inner = width // 3
    pf[:, 1664:1792] = jnp.zeros((2 * places, 128), F32)
    project(0, a)
    exchange(0)
    def relay_back(target):
        @pl.when(target != y)
        def _():
            z_back(target).wait_recv()
            y_back_relay(target).start()

    each(0, 8, relay_back)
    z_back_home().wait_recv()

    def relay_end(j):
        copy = send(
            zro.at[0], mixb.at[1, 0], yos.at[1, j], yor.at[1, j], (f, a * 8 + lax.rem(y + j, 8))
        )
        copy.wait_recv()
        copy.wait_send()

    each(1, 8, relay_end)
    each(1, 8, lambda j: y_back(j).wait_send())

    project(1, far)
    exchange(1)
    for kind in range(2):
        for j in ORDER:
            relay_level(kind, 6 - j)

    def gather(kind, level):
        each(1, 8, lambda j: row_arrival(kind, level, j).wait_recv())
        for half_row in range(2):
            parts = [rb[kind, 8 * level + 4 * half_row + t].astype(F32) for t in range(4)]
            start = pl.multiple_of(kind * 96 + 16 * level + 8 * half_row, 8)
            pf[pl.ds(start, 8), :] = jnp.concatenate(parts, axis=0)

    for kind in range(2):
        for j in (0,) + ORDER:
            gather(kind, lax.rem(z + 6 - j, 6))

    by_place = one_hot(
        lambda r: (lax.rem(r, 96) // 48) * 96 + 2 * lax.rem(r, 48) + r // 96
    )
    to_group = one_hot(
        lambda r: lax.rem(r, 2) * 96 + lax.rem(r // 2, 2) * 48 + r // 4
    )
    to_rows = one_hot(
        lambda r: 4 * (lax.rem(r, 96) // 2) + 2 * (r // 96) + lax.rem(r, 2)
    )
    rows = jnp.dot(by_place, pf[...].astype(BF), preferred_element_type=F32).astype(BF)
    lanes256 = lax.broadcasted_iota(jnp.int32, (96, 256), 1)
    tm[...] = jnp.zeros(tm.shape, F32)
    for p in range(2):
        block = rows[p * 96 : p * 96 + 96]
        for head in range(T_HEADS):
            start = head * HEAD
            queries = block[:, start : start + HEAD]
            keys = block[:, inner + start : inner + start + HEAD]
            window = min((start // 128) * 128, 384)
            scores = lax.dot_general(
                queries, keys, (((1,), (1,)), ((), ())), preferred_element_type=F32
            )
            largest = jnp.max(scores, axis=1, keepdims=True)
            expons = jnp.exp2((scores - largest) * EXP2_SCALE)
            totals = jnp.sum(expons, axis=1, keepdims=True)
            vals = block[:, 2 * inner + window : min(2 * inner + window + 256, 1792)]
            product = jnp.dot(expons.astype(BF), vals, preferred_element_type=F32) / totals
            near = lanes256[:, : vals.shape[1]] + window
            held = (near >= start) & (near < start + HEAD)
            spot = (slice(p * 96, p * 96 + 96), slice(window, window + vals.shape[1]))
            tm[spot] = jnp.where(held, product, tm[spot])

    pf[:, 0:640] = jnp.dot(to_group, tm[...].astype(BF), preferred_element_type=F32)

    def cut_back(g):
        both = pf[pl.ds(pl.multiple_of(8 * g, 8), 8), 0:640]
        sb2[2 * g] = both[0:4].astype(BF)
        sb2[2 * g + 1] = both[4:8].astype(BF)

    each(0, 24, cut_back)

    def level_home(j):
        level = lax.rem(z + j, 6)
        return send(
            sb2.at[pl.ds(8 * level, 8)], zx2.at[z], us.at[level], ur.at[z], peer(kme, level)
        )

    def level_home_arrival(level):
        return send(
            sb2.at[pl.ds(0, 8)], zx2.at[level], us.at[level], ur.at[level], peer(kme, level)
        )

    def row_home(level, j, own):
        k = lax.rem(kme + j, 8)
        source = sb2.at[8 * z + k] if own else zx2.at[level, k]
        return send(
            source, rb2.at[level * 8 + kme], ws.at[level, k], wr.at[level, kme], peer(k, z)
        )

    def row_home_arrival(level, j):
        k = lax.rem(kme + j, 8)
        return send(
            sb2.at[0], rb2.at[level * 8 + k], ws.at[level, k], wr.at[level, k], peer(k, z)
        )

    for j in ORDER:
        level_home(j).start()
    each(1, 8, lambda j: row_home(z, j, True).start())
    rb2[8 * z + kme] = sb2[8 * z + kme]
    for j in ORDER:
        level = lax.rem(z + 6 - j, 6)
        level_home_arrival(level).wait_recv()
        each(1, 8, lambda i: row_home(level, i, False).start())
        rb2[8 * level + kme] = zx2[level, kme]

    def gather_back(level):
        each(1, 8, lambda j: row_home_arrival(level, j).wait_recv())
        for part in range(4):
            start = pl.multiple_of(32 * level + 8 * part, 8)
            pair = 8 * level + 2 * part
            pf[pl.ds(start, 8), 0:640] = jnp.concatenate(
                [rb2[pair].astype(F32), rb2[pair + 1].astype(F32)], axis=0
            )

    for j in (0,) + ORDER:
        gather_back(lax.rem(z + 6 - j, 6))
    final = jnp.dot(to_rows, pf[:, 0:640].astype(BF), preferred_element_type=F32)
    mix_out[a] = final[0:96, 0:inner].astype(BF)
    mix_out[far] = final[96:192, 0:inner].astype(BF)

    for j in ORDER:
        for kind in range(2):
            level_copy(kind, j).wait_send()
        level_home(j).wait_send()

    def drain(level):
        def one(j):
            for kind in range(2):
                row_copy(kind, level, j, False).wait_send()
            row_home(level, j, False).wait_send()

        each(1, 8, one)

    each(0, 6, drain)
    each(0, 8, lambda target: z_back(target).wait_send())
    for t in range(3):
        z_home(t).wait_send()
        each(1, 8, lambda j: z_copy(t, j).wait_send())
        each(1, 8, lambda j: y_copy(t, j).wait_send())
        each(1, 8, lambda j: y_relay(t, j).wait_send())


def per_device(residual_in, q_spatial, k_spatial, v_spatial, w_out, modulation, w_temporal):
    frames, places, features = residual_in.shape
    half = places // 2
    total = 16 * places
    width = w_temporal.shape[1]
    vmem = pl.BlockSpec(memory_space=pltpu.VMEM)
    hbm = pl.BlockSpec(memory_space=pl.ANY)
    dma = pltpu.SemaphoreType.DMA
    local = (frames, places, features)
    return pl.pallas_call(
        block_kernel,
        out_shape=(
            jax.ShapeDtypeStruct(local, BF),
            jax.ShapeDtypeStruct((frames, places, width // 3), BF),
        ),
        in_specs=[hbm] * 5 + [vmem, hbm],
        out_specs=(vmem, vmem),
        scratch_shapes=[
            pltpu.VMEM(local, BF),
            pltpu.VMEM(local, BF),
            pltpu.VMEM(local, BF),
            pltpu.VMEM(local, BF),
            pltpu.VMEM((features, features), BF),
            pltpu.VMEM((width, features), BF),
            pltpu.VMEM((2, 8, places + half, 128), BF),
            pltpu.VMEM((2, 8, places, 128), BF),
            pltpu.VMEM((2, 8, places, 128), BF),
            pltpu.VMEM((8, places + half, 128), BF),
            pltpu.VMEM((8, places, 128), BF),
            pltpu.VMEM((8, places, 128), BF),
            pltpu.VMEM((16, places + half, 128), BF),
            pltpu.VMEM((16, places, 128), BF),
            pltpu.VMEM((16, places, 128), BF),
            pltpu.VMEM((total, 256), BF),
            pltpu.VMEM((total, 128), BF),
            pltpu.VMEM((total, 256), BF),
            pltpu.VMEM((total, 256), BF),
            pltpu.VMEM((2, total, total), BF),
            pltpu.VMEM((16, places + 16, 128), BF),
            pltpu.VMEM((8, places + 16, 128), BF),
            pltpu.VMEM((2, 8, places + 16, 128), BF),
            pltpu.VMEM((2, places, features), BF),
            pltpu.VMEM((2 * places, 1792), F32),
            pltpu.VMEM((2, 48, 2, 1792), BF),
            pltpu.VMEM((2, 6, 8, 2, 1792), BF),
            pltpu.VMEM((2, 48, 2, 1792), BF),
            pltpu.VMEM((2 * places, 640), F32),
            pltpu.VMEM((48, 4, 640), BF),
            pltpu.VMEM((6, 8, 4, 640), BF),
            pltpu.VMEM((48, 4, 640), BF),
            dma((21,)),
            dma((3, 8)), dma((3, 8)), dma((2, 3, 8)), dma((2, 3, 8)),
            dma((8,)), dma((8,)), dma((2, 8)), dma((2, 8)),
            dma((2, 6)), dma((2, 6)), dma((2, 6, 8)), dma((2, 6, 8)),
            dma((6,)), dma((6,)), dma((6, 8)), dma((6, 8)),
        ],
        compiler_params=pltpu.CompilerParams(
            collective_id=1, has_side_effects=True, vmem_limit_bytes=52 << 20
        ),
        name="block",
    )(residual_in, q_spatial, k_spatial, v_spatial, w_out, modulation, w_temporal.T)


def solution(mesh):
    return jax.shard_map(
        per_device,
        mesh=mesh,
        in_specs=(
            P("frame", "space", None),
            P("frame", "space", None),
            P("frame", "space", None),
            P("frame", "space", None),
            P(),
            P(),
            P(),
        ),
        out_specs=(P("frame", "space", None), P("frame", "space", None)),
        check_vma=False,
    )
```

```python
import functools
import math

import jax
import jax.numpy as jnp
from jax import lax
from jax.experimental import pallas as pl
from jax.experimental.pallas import tpu as pltpu
from jax.sharding import PartitionSpec as P

MESH = pl.DeviceIdType.MESH
HEAD = 72
T_HEADS = 8
BF = jnp.bfloat16
F32 = jnp.float32
ORDER = (3, 2, 4, 1, 5)
EXP2_SCALE = math.log2(math.e) / math.sqrt(HEAD)


def lane_iota(rows):
    return lax.broadcasted_iota(jnp.int32, (rows, 128), 1)


def roll_lanes(x, shift):
    shift = shift % 128
    if shift == 0:
        return x
    return pltpu.roll(x, shift, axis=1)


def send(src, dst, ssem, rsem, device):
    return pltpu.make_async_remote_copy(
        src_ref=src, dst_ref=dst, send_sem=ssem, recv_sem=rsem, device_id=device, device_id_type=MESH
    )


def one_hot(rows_of):
    size = 192
    row = lax.broadcasted_iota(jnp.int32, (size, size), 0)
    column = lax.broadcasted_iota(jnp.int32, (size, size), 1)
    return jnp.where(column == rows_of(row), 1.0, 0.0).astype(BF)


def block_kernel(
    res_hbm, q_hbm, k_hbm, v_hbm, wo_hbm, mod_ref, wt_hbm, res_out, mix_out,
    q_ref, k_ref, v_ref, res_ref, wp, wt,
    sba, sbb, zra, zrb, fa, fb, qs, ks, vs, ob, zro, mixb,
    am, pf, sb, zx, rb, tm, sb2, zx2, rb2,
    ld, zs, zr, ys, yr, zos, zor, yos, yor, ts, tr, xs, xr, us, ur, ws, wr,
):
    f = lax.axis_index("frame")
    s = lax.axis_index("space")
    a = s // 8
    y = lax.rem(s, 8)
    far = 1 - a
    partner = (f, far * 8 + y)
    places = q_ref.shape[1]
    core = lax.rem(f, 2)
    z = lax.rem(f // 2, 6)
    kme = (f // 12) * 2 + core

    def peer(k, level):
        return (((k // 2) * 6 + level) * 2 + lax.rem(k, 2), s)

    loads = [
        pltpu.make_async_copy(k_hbm, k_ref, ld.at[0]),
        pltpu.make_async_copy(q_hbm, q_ref, ld.at[1]),
        pltpu.make_async_copy(v_hbm, v_ref, ld.at[2]),
        pltpu.make_async_copy(res_hbm, res_ref, ld.at[3]),
        pltpu.make_async_copy(wt_hbm, wt, ld.at[4]),
    ]
    for head in range(16):
        loads.append(
            pltpu.make_async_copy(
                wo_hbm.at[pl.ds(HEAD * head, HEAD)],
                wp.at[pl.ds(128 * head, HEAD)],
                ld.at[5 + head],
            )
        )
    for load in loads[:3]:
        load.start()
    half = places // 2

    barrier = pltpu.get_barrier_semaphore()
    pl.semaphore_signal(barrier, inc=1, device_id=partner, device_id_type=MESH)

    def greet(j, carry):
        pl.semaphore_signal(
            barrier, inc=1, device_id=(f, a * 8 + lax.rem(y + j, 8)), device_id_type=MESH
        )
        return carry

    lax.fori_loop(1, 8, greet, 0)

    def greet_level(j, carry):
        pl.semaphore_signal(
            barrier, inc=1, device_id=peer(kme, lax.rem(z + j, 6)), device_id_type=MESH
        )
        return carry

    lax.fori_loop(1, 6, greet_level, 0)

    def greet_row(j, carry):
        pl.semaphore_signal(
            barrier, inc=1, device_id=peer(lax.rem(kme + j, 8), z), device_id_type=MESH
        )
        return carry

    lax.fori_loop(1, 8, greet_row, 0)
    for load in loads[:3]:
        load.wait()
    for load in loads[3:]:
        load.start()
    for head in range(16):
        wp[128 * head + HEAD : 128 * head + 128] = jnp.zeros((128 - HEAD, wp.shape[1]), BF)

    lanes = lane_iota(places)
    half_lanes = lane_iota(half)

    def tile(ref, fr, index):
        return ref[fr, :, 128 * index : 128 * index + 128].astype(F32)

    def piece(ref, fr, column, count, target):
        index, offset = column // 128, column % 128
        value = tile(ref, fr, index)
        if offset + count > 128:
            value = jnp.where(lanes >= offset, value, tile(ref, fr, index + 1))
        return roll_lanes(value, target - offset)

    def pack_first(fr):
        for pair in range(8):
            c = 144 * pair
            one = jnp.where(
                lanes < 72, piece(q_ref, fr, c, 72, 0), piece(k_ref, fr, c, 56, 72)
            )
            two = jnp.where(
                lanes < 16,
                piece(k_ref, fr, c + 56, 16, 0),
                jnp.where(
                    lanes < 88, piece(v_ref, fr, c, 72, 16), piece(q_ref, fr, c + 72, 40, 88)
                ),
            )
            sba[fr, pair, 0:places] = one.astype(BF)
            sba[fr, pair, places : 2 * places] = two.astype(BF)

    def pack_second(fr):
        for pair in range(8):
            c = 144 * pair + 72
            three = jnp.where(
                lanes < 32,
                piece(q_ref, fr, c + 40, 32, 0),
                jnp.where(
                    lanes < 104, piece(k_ref, fr, c, 72, 32), piece(v_ref, fr, c, 24, 104)
                ),
            )
            left = piece(v_ref, fr, c + 24, 48, 0)
            joined = jnp.where(half_lanes < 64, left[0:half], roll_lanes(left[half:places], 64))
            sbb[fr, pair, 0:places] = three.astype(BF)
            sbb[fr, pair, places : places + half] = joined.astype(BF)

    sent = ((sba, zra, fa), (sbb, zrb, fb))

    def z_copy(t, j):
        buf, relay, final = sent[t]
        target = lax.rem(y + j, 8)
        return send(buf.at[far, target], relay.at[j], zs.at[t, j], zr.at[t, j], partner)

    def z_home(t):
        buf, relay, final = sent[t]
        return send(buf.at[far, y], final.at[s], zs.at[t, 0], zr.at[t, 0], partner)

    def y_copy(t, j):
        buf, relay, final = sent[t]
        target = lax.rem(y + j, 8)
        return send(
            buf.at[a, target], final.at[s], ys.at[0, t, j], yr.at[0, t, j], (f, a * 8 + target)
        )

    def y_relay(t, j):
        buf, relay, final = sent[t]
        target = lax.rem(y + j, 8)
        return send(
            relay.at[j], final.at[far * 8 + y], ys.at[1, t, j], yr.at[1, t, j],
            (f, a * 8 + target),
        )

    def each(low, high, body):
        def step(j, carry):
            body(j)
            return carry

        lax.fori_loop(low, high, step, 0)

    pack_first(far)
    pl.semaphore_wait(barrier, 20)

    def z_start(t):
        each(1, 8, lambda j: z_copy(t, j).start())
        z_home(t).start()

    def y_start(t):
        each(1, 8, lambda j: y_copy(t, j).start())

    z_start(0)
    pack_second(far)
    z_start(1)
    pack_first(a)
    y_start(0)
    pack_second(a)
    y_start(1)
    fa[s] = sba[a, y]
    fb[s] = sbb[a, y]

    def forward(t, j):
        z_copy(t, j).wait_recv()
        y_relay(t, j).start()

    def settle(t):
        z_home(t).wait_recv()
        each(1, 8, lambda j: y_copy(t, j).wait_recv())
        each(1, 8, lambda j: y_relay(t, j).wait_recv())

    big = 4 * places
    zero = jnp.zeros((places, 128), F32)
    ones = jnp.where(lanes == HEAD, 1.0, zero)

    def rows_of(block):
        return pl.ds(pl.multiple_of(block * places, places), places)

    def spread_first(block):
        rows = rows_of(block)
        one = fa[block, 0:places].astype(F32)
        two = fa[block, places : 2 * places].astype(F32)
        qs[0, rows, :] = fa[block, 0:places]
        ks[0, rows, :] = jnp.where(
            lanes < 56, roll_lanes(one, -72), jnp.where(lanes < HEAD, roll_lanes(two, 56), zero)
        ).astype(BF)
        vs[0, rows, :] = jnp.where(lanes < HEAD, roll_lanes(two, -16), ones).astype(BF)

    def spread_second(block):
        rows = rows_of(block)
        two = fa[block, places : 2 * places].astype(F32)
        three = fb[block, 0:places].astype(F32)
        packed = fb[block, places : places + half].astype(F32)
        left = jnp.concatenate([packed, roll_lanes(packed, 64)], axis=0)
        qs[1, rows, :] = jnp.where(lanes < 40, roll_lanes(two, -88), roll_lanes(three, 40)).astype(BF)
        ks[1, rows, :] = jnp.where(lanes < HEAD, roll_lanes(three, -32), zero).astype(BF)
        vs[1, rows, :] = jnp.where(
            lanes < 24, roll_lanes(three, -104), jnp.where(lanes < HEAD, roll_lanes(left, 24), ones)
        ).astype(BF)

    lanes40 = lane_iota(40)
    lanes16 = lane_iota(16)

    def attend(head, first):
        rows = pl.ds(pl.multiple_of(first * places, places), big)
        scores = lax.dot_general(
            qs[head, rows, :], ks[head], (((1,), (1,)), ((), ())), preferred_element_type=F32
        )
        largest = jnp.max(scores, axis=1, keepdims=True)
        weights = jnp.exp2((scores - largest) * EXP2_SCALE).astype(BF)
        product = jnp.dot(weights, vs[head], preferred_element_type=F32)
        mixed = product * (1.0 / product[:, HEAD : HEAD + 1])
        for part in range(4):
            val = mixed[part * places : (part + 1) * places]
            top = jnp.where(lanes40 < HEAD, val[0:40], roll_lanes(val[56:96], 72))
            last = jnp.concatenate([val[88:96], val[88:96]], axis=0)
            low = jnp.where(
                lanes16 < HEAD,
                val[40:56],
                jnp.where(
                    lanes16 < 88,
                    roll_lanes(val[56:72], 16),
                    jnp.where(lanes16 < 104, roll_lanes(val[72:88], 32), roll_lanes(last, 48)),
                ),
            )
            ob[head, first + part, 0:40] = top.astype(BF)
            ob[head, first + part, 40:56] = low.astype(BF)

    def z_back(head, target):
        return send(
            ob.at[head, far * 8 + target], zro.at[head, target], zos.at[head, target],
            zor.at[head, target], partner,
        )

    def z_back_home(head):
        return send(
            ob.at[head, far * 8 + y], mixb.at[1, head, y], zos.at[head, y], zor.at[head, y], partner
        )

    def y_back(head, j):
        target = lax.rem(y + j, 8)
        return send(
            ob.at[head, a * 8 + target], mixb.at[0, head, y], yos.at[head, 0, j],
            yor.at[head, 0, j], (f, a * 8 + target),
        )

    def y_back_relay(head, target):
        j = lax.rem(target + 8 - y, 8)
        return send(
            zro.at[head, target], mixb.at[1, head, y], yos.at[head, 1, j], yor.at[head, 1, j],
            (f, a * 8 + target),
        )

    def y_back_arrival(head, which, j):
        source = lax.rem(y + 8 - j, 8)
        return send(
            zro.at[head, 0], mixb.at[which, head, source], yos.at[head, which, j],
            yor.at[head, which, j], (f, a * 8 + lax.rem(y + j, 8)),
        )

    def attend_all(head):
        def z_back_start(target):
            @pl.when(target != y)
            def _():
                z_back(head, target).start()

            @pl.when(target == y)
            def _():
                z_back_home(head).start()

        def far_part(step):
            attend(head, far * 8 + 4 * step)
            each(4 * step, 4 * step + 4, z_back_start)

        each(0, 2, far_part)
        each(0, 2, lambda step: attend(head, a * 8 + 4 * step))
        each(1, 8, lambda j: y_back(head, j).start())
        mixb[0, head, y] = ob[head, s]

    def relay_back(head):
        def one(target):
            @pl.when(target != y)
            def _():
                z_back(head, target).wait_recv()
                y_back_relay(head, target).start()

        each(0, 8, one)

    each(1, 8, lambda j: forward(0, j))
    settle(0)
    each(0, 16, spread_first)
    attend_all(0)
    each(1, 8, lambda j: forward(1, j))
    settle(1)
    each(0, 16, spread_second)
    attend_all(1)
    relay_back(0)
    for load in loads[3:]:
        load.wait()

    def project(kind, frame):
        for pair in range(8):
            for head in range(2):
                spot = slice(256 * pair + 128 * head, 256 * pair + 128 * head + 128)
                block = mixb[kind, head, pair].astype(F32)
                tail = block[40:56]
                low = jnp.concatenate(
                    [roll_lanes(tail, -16), roll_lanes(tail, -32), roll_lanes(tail[0:8], -48)],
                    axis=0,
                )
                am[kind, 0:56, spot] = mixb[kind, head, pair]
                am[kind, 56:96, spot] = jnp.where(
                    lanes40 < 56, roll_lanes(block[0:40], -72), low
                ).astype(BF)
        branch = jnp.dot(am[kind], wp[...], preferred_element_type=F32)
        res = (res_ref[frame].astype(F32) + mod_ref[2:3, :] * branch).astype(BF)
        res_out[frame] = res
        values = res.astype(F32)
        center = jnp.mean(values, axis=1, keepdims=True)
        moved = values - center
        deviation = jnp.mean(moved * moved, axis=1, keepdims=True)
        normed = moved * lax.rsqrt(deviation + 1e-06) * (1.0 + mod_ref[1:2, :]) + mod_ref[0:1, :]
        pf[0:places, 0:width] = lax.dot_general(
            normed.astype(BF), wt[...], (((1,), (1,)), ((), ())), preferred_element_type=F32
        )

        def cut(g):
            eight = pf[pl.ds(pl.multiple_of(8 * g, 8), 8), :]
            for t in range(4):
                sb[kind, 4 * g + t] = eight[2 * t : 2 * t + 2].astype(BF)

        each(0, places // 8, cut)

    def level_copy(kind, j):
        level = lax.rem(z + j, 6)
        return send(
            sb.at[kind, pl.ds(8 * level, 8)], zx.at[kind, z], ts.at[kind, level], tr.at[kind, z],
            peer(kme, level),
        )

    def level_arrival(kind, level):
        return send(
            sb.at[kind, pl.ds(0, 8)], zx.at[kind, level], ts.at[kind, level], tr.at[kind, level],
            peer(kme, level),
        )

    def row_copy(kind, level, j, own):
        k = lax.rem(kme + j, 8)
        source = sb.at[kind, 8 * z + k] if own else zx.at[kind, level, k]
        return send(
            source, rb.at[kind, level * 8 + kme], xs.at[kind, level, k], xr.at[kind, level, kme],
            peer(k, z),
        )

    def row_arrival(kind, level, j):
        k = lax.rem(kme + j, 8)
        return send(
            sb.at[kind, 0], rb.at[kind, level * 8 + k], xs.at[kind, level, k],
            xr.at[kind, level, k], peer(k, z),
        )

    def exchange(kind):
        for j in ORDER:
            level_copy(kind, j).start()
        each(1, 8, lambda j: row_copy(kind, z, j, True).start())
        rb[kind, 8 * z + kme] = sb[kind, 8 * z + kme]

    def relay_level(kind, j):
        level = lax.rem(z + j, 6)
        level_arrival(kind, level).wait_recv()
        each(1, 8, lambda i: row_copy(kind, level, i, False).start())
        rb[kind, 8 * level + kme] = zx[kind, level, kme]

    for head in range(2):
        each(1, 8, lambda j: y_back_arrival(head, 0, j).wait_recv())
    width = wt.shape[0]
    inner = width // 3
    pf[:, 1664:1792] = jnp.zeros((2 * places, 128), F32)
    project(0, a)
    exchange(0)
    relay_back(1)
    for head in range(2):
        z_back_home(head).wait_recv()
        each(1, 8, lambda j: y_back_arrival(head, 1, j).wait_recv())
    project(1, far)
    exchange(1)
    for kind in range(2):
        for j in ORDER:
            relay_level(kind, 6 - j)

    def gather(kind, level):
        each(1, 8, lambda j: row_arrival(kind, level, j).wait_recv())
        for half_row in range(2):
            parts = [rb[kind, 8 * level + 4 * half_row + t].astype(F32) for t in range(4)]
            start = pl.multiple_of(kind * 96 + 16 * level + 8 * half_row, 8)
            pf[pl.ds(start, 8), :] = jnp.concatenate(parts, axis=0)

    for kind in range(2):
        for j in (0,) + ORDER:
            gather(kind, lax.rem(z + 6 - j, 6))

    by_place = one_hot(
        lambda r: (lax.rem(r, 96) // 48) * 96 + 2 * lax.rem(r, 48) + r // 96
    )
    to_group = one_hot(
        lambda r: lax.rem(r, 2) * 96 + lax.rem(r // 2, 2) * 48 + r // 4
    )
    to_rows = one_hot(
        lambda r: 4 * (lax.rem(r, 96) // 2) + 2 * (r // 96) + lax.rem(r, 2)
    )
    rows = jnp.dot(by_place, pf[...].astype(BF), preferred_element_type=F32).astype(BF)
    lanes256 = lax.broadcasted_iota(jnp.int32, (96, 256), 1)
    tm[...] = jnp.zeros(tm.shape, F32)
    for p in range(2):
        block = rows[p * 96 : p * 96 + 96]
        for head in range(T_HEADS):
            start = head * HEAD
            queries = block[:, start : start + HEAD]
            keys = block[:, inner + start : inner + start + HEAD]
            window = min((start // 128) * 128, 384)
            scores = lax.dot_general(
                queries, keys, (((1,), (1,)), ((), ())), preferred_element_type=F32
            )
            largest = jnp.max(scores, axis=1, keepdims=True)
            expons = jnp.exp2((scores - largest) * EXP2_SCALE)
            totals = jnp.sum(expons, axis=1, keepdims=True)
            vals = block[:, 2 * inner + window : min(2 * inner + window + 256, 1792)]
            product = jnp.dot(expons.astype(BF), vals, preferred_element_type=F32) / totals
            near = lanes256[:, : vals.shape[1]] + window
            held = (near >= start) & (near < start + HEAD)
            spot = (slice(p * 96, p * 96 + 96), slice(window, window + vals.shape[1]))
            tm[spot] = jnp.where(held, product, tm[spot])

    pf[:, 0:640] = jnp.dot(to_group, tm[...].astype(BF), preferred_element_type=F32)

    def cut_back(g):
        both = pf[pl.ds(pl.multiple_of(8 * g, 8), 8), 0:640]
        sb2[2 * g] = both[0:4].astype(BF)
        sb2[2 * g + 1] = both[4:8].astype(BF)

    each(0, 24, cut_back)

    def level_home(j):
        level = lax.rem(z + j, 6)
        return send(
            sb2.at[pl.ds(8 * level, 8)], zx2.at[z], us.at[level], ur.at[z], peer(kme, level)
        )

    def level_home_arrival(level):
        return send(
            sb2.at[pl.ds(0, 8)], zx2.at[level], us.at[level], ur.at[level], peer(kme, level)
        )

    def row_home(level, j, own):
        k = lax.rem(kme + j, 8)
        source = sb2.at[8 * z + k] if own else zx2.at[level, k]
        return send(
            source, rb2.at[level * 8 + kme], ws.at[level, k], wr.at[level, kme], peer(k, z)
        )

    def row_home_arrival(level, j):
        k = lax.rem(kme + j, 8)
        return send(
            sb2.at[0], rb2.at[level * 8 + k], ws.at[level, k], wr.at[level, k], peer(k, z)
        )

    for j in ORDER:
        level_home(j).start()
    each(1, 8, lambda j: row_home(z, j, True).start())
    rb2[8 * z + kme] = sb2[8 * z + kme]
    for j in ORDER:
        level = lax.rem(z + 6 - j, 6)
        level_home_arrival(level).wait_recv()
        each(1, 8, lambda i: row_home(level, i, False).start())
        rb2[8 * level + kme] = zx2[level, kme]

    def gather_back(level):
        each(1, 8, lambda j: row_home_arrival(level, j).wait_recv())
        for part in range(4):
            start = pl.multiple_of(32 * level + 8 * part, 8)
            pair = 8 * level + 2 * part
            pf[pl.ds(start, 8), 0:640] = jnp.concatenate(
                [rb2[pair].astype(F32), rb2[pair + 1].astype(F32)], axis=0
            )

    for j in (0,) + ORDER:
        gather_back(lax.rem(z + 6 - j, 6))
    final = jnp.dot(to_rows, pf[:, 0:640].astype(BF), preferred_element_type=F32)
    mix_out[a] = final[0:96, 0:inner].astype(BF)
    mix_out[far] = final[96:192, 0:inner].astype(BF)

    for j in ORDER:
        for kind in range(2):
            level_copy(kind, j).wait_send()
        level_home(j).wait_send()

    def drain(level):
        def one(j):
            for kind in range(2):
                row_copy(kind, level, j, False).wait_send()
            row_home(level, j, False).wait_send()

        each(1, 8, one)

    each(0, 6, drain)
    for head in range(2):
        each(0, 8, lambda target: z_back(head, target).wait_send())
        for which in range(2):
            each(1, 8, lambda j: y_back_arrival(head, which, j).wait_send())
    for t in range(2):
        z_home(t).wait_send()
        each(1, 8, lambda j: z_copy(t, j).wait_send())
        each(1, 8, lambda j: y_copy(t, j).wait_send())
        each(1, 8, lambda j: y_relay(t, j).wait_send())


def per_device(residual_in, q_spatial, k_spatial, v_spatial, w_out, modulation, w_temporal):
    frames, places, features = residual_in.shape
    half = places // 2
    total = 16 * places
    width = w_temporal.shape[1]
    vmem = pl.BlockSpec(memory_space=pltpu.VMEM)
    hbm = pl.BlockSpec(memory_space=pl.ANY)
    dma = pltpu.SemaphoreType.DMA
    local = (frames, places, features)
    return pl.pallas_call(
        block_kernel,
        out_shape=(
            jax.ShapeDtypeStruct(local, BF),
            jax.ShapeDtypeStruct((frames, places, width // 3), BF),
        ),
        in_specs=[hbm] * 5 + [vmem, hbm],
        out_specs=(vmem, vmem),
        scratch_shapes=[
            pltpu.VMEM(local, BF),
            pltpu.VMEM(local, BF),
            pltpu.VMEM(local, BF),
            pltpu.VMEM(local, BF),
            pltpu.VMEM((16 * 128, features), BF),
            pltpu.VMEM((width, features), BF),
            pltpu.VMEM((2, 8, 2 * places, 128), BF),
            pltpu.VMEM((2, 8, places + half, 128), BF),
            pltpu.VMEM((8, 2 * places, 128), BF),
            pltpu.VMEM((8, places + half, 128), BF),
            pltpu.VMEM((16, 2 * places, 128), BF),
            pltpu.VMEM((16, places + half, 128), BF),
            pltpu.VMEM((2, total, 128), BF),
            pltpu.VMEM((2, total, 128), BF),
            pltpu.VMEM((2, total, 128), BF),
            pltpu.VMEM((2, 16, 56, 128), BF),
            pltpu.VMEM((2, 8, 56, 128), BF),
            pltpu.VMEM((2, 2, 8, 56, 128), BF),
            pltpu.VMEM((2, places, 16 * 128), BF),
            pltpu.VMEM((2 * places, 1792), F32),
            pltpu.VMEM((2, 48, 2, 1792), BF),
            pltpu.VMEM((2, 6, 8, 2, 1792), BF),
            pltpu.VMEM((2, 48, 2, 1792), BF),
            pltpu.VMEM((2 * places, 640), F32),
            pltpu.VMEM((48, 4, 640), BF),
            pltpu.VMEM((6, 8, 4, 640), BF),
            pltpu.VMEM((48, 4, 640), BF),
            dma((21,)),
            dma((2, 8)), dma((2, 8)), dma((2, 2, 8)), dma((2, 2, 8)),
            dma((2, 8)), dma((2, 8)), dma((2, 2, 8)), dma((2, 2, 8)),
            dma((2, 6)), dma((2, 6)), dma((2, 6, 8)), dma((2, 6, 8)),
            dma((6,)), dma((6,)), dma((6, 8)), dma((6, 8)),
        ],
        compiler_params=pltpu.CompilerParams(
            collective_id=1, has_side_effects=True, vmem_limit_bytes=67043328
        ),
        name="block",
    )(residual_in, q_spatial, k_spatial, v_spatial, w_out, modulation, w_temporal.T)


def solution(mesh):
    return jax.shard_map(
        per_device,
        mesh=mesh,
        in_specs=(
            P("frame", "space", None),
            P("frame", "space", None),
            P("frame", "space", None),
            P("frame", "space", None),
            P(),
            P(),
            P(),
        ),
        out_specs=(P("frame", "space", None), P("frame", "space", None)),
        check_vma=False,
    )
```

```python
import functools
import math

import jax
import jax.numpy as jnp
from jax import lax
from jax.experimental import pallas as pl
from jax.experimental.pallas import tpu as pltpu
from jax.sharding import PartitionSpec as P

MESH = pl.DeviceIdType.MESH
HEAD = 72
T_HEADS = 8
BF = jnp.bfloat16
F32 = jnp.float32
ORDER = (1, 2, 3, 4, 5)
EXP2_SCALE = math.log2(math.e) / math.sqrt(HEAD)


def lane_iota(rows):
    return lax.broadcasted_iota(jnp.int32, (rows, 128), 1)


def roll_lanes(x, shift):
    shift = shift % 128
    if shift == 0:
        return x
    return pltpu.roll(x, shift, axis=1)


def send(src, dst, ssem, rsem, device):
    return pltpu.make_async_remote_copy(
        src_ref=src, dst_ref=dst, send_sem=ssem, recv_sem=rsem, device_id=device, device_id_type=MESH
    )


def one_hot(rows_of):
    size = 192
    row = lax.broadcasted_iota(jnp.int32, (size, size), 0)
    column = lax.broadcasted_iota(jnp.int32, (size, size), 1)
    return jnp.where(column == rows_of(row), 1.0, 0.0).astype(BF)


def block_kernel(
    res_hbm, q_hbm, k_hbm, v_hbm, wo_hbm, mod_ref, wt_hbm, res_out, mix_out,
    q_ref, k_ref, v_ref, res_ref, wp, wt,
    sbk, sbq, sbv, zrk, zrq, zrv, fk, fq, fv, qs, k0, k1, vs, pr, ob, zro, mixb,
    am, pf, sb, zx, rb, tm, sb2, zx2, rb2,
    ld, zs, zr, ys, yr, zos, zor, yos, yor, ts, tr, xs, xr, us, ur, ws, wr,
):
    f = lax.axis_index("frame")
    s = lax.axis_index("space")
    a = s // 8
    y = lax.rem(s, 8)
    far = 1 - a
    partner = (f, far * 8 + y)
    places = q_ref.shape[1]
    core = lax.rem(f, 2)
    z = lax.rem(f // 2, 6)
    kme = (f // 12) * 2 + core

    def peer(k, level):
        return (((k // 2) * 6 + level) * 2 + lax.rem(k, 2), s)

    loads = [
        pltpu.make_async_copy(k_hbm, k_ref, ld.at[0]),
        pltpu.make_async_copy(q_hbm, q_ref, ld.at[1]),
        pltpu.make_async_copy(v_hbm, v_ref, ld.at[2]),
        pltpu.make_async_copy(res_hbm, res_ref, ld.at[3]),
        pltpu.make_async_copy(wt_hbm, wt, ld.at[4]),
    ]
    for pair in range(8):
        loads.append(
            pltpu.make_async_copy(
                wo_hbm.at[pl.ds(144 * pair, 128)], wp.at[pl.ds(128 * pair, 128)], ld.at[5 + 2 * pair]
            )
        )
        loads.append(
            pltpu.make_async_copy(
                wo_hbm.at[pl.ds(144 * pair + 128, 16)],
                wp.at[pl.ds(1024 + 16 * pair, 16)],
                ld.at[6 + 2 * pair],
            )
        )
    for load in loads[:3]:
        load.start()
    half = places // 2

    barrier = pltpu.get_barrier_semaphore()
    pl.semaphore_signal(barrier, inc=1, device_id=partner, device_id_type=MESH)

    def greet(j, carry):
        pl.semaphore_signal(
            barrier, inc=1, device_id=(f, a * 8 + lax.rem(y + j, 8)), device_id_type=MESH
        )
        return carry

    lax.fori_loop(1, 8, greet, 0)

    def greet_level(j, carry):
        pl.semaphore_signal(
            barrier, inc=1, device_id=peer(kme, lax.rem(z + j, 6)), device_id_type=MESH
        )
        return carry

    lax.fori_loop(1, 6, greet_level, 0)

    def greet_row(j, carry):
        pl.semaphore_signal(
            barrier, inc=1, device_id=peer(lax.rem(kme + j, 8), z), device_id_type=MESH
        )
        return carry

    lax.fori_loop(1, 8, greet_row, 0)
    for load in loads[:3]:
        load.wait()
    for load in loads[3:]:
        load.start()

    lanes = lane_iota(places)
    half_lanes = lane_iota(half)

    def tile(ref, fr, index):
        return ref[fr, :, 128 * index : 128 * index + 128].astype(F32)

    def main_of(ref, fr, pair):
        low = tile(ref, fr, pair)
        if pair == 0:
            return low.astype(BF)
        high = tile(ref, fr, pair + 1)
        return roll_lanes(jnp.where(lanes >= 16 * pair, low, high), -16 * pair).astype(BF)

    def pack_k(fr):
        for pair in range(8):
            sbk[fr, pair, 0:places] = main_of(k_ref, fr, pair)
            left = jnp.where(
                lanes < 16,
                roll_lanes(tile(k_ref, fr, pair + 1), -16 * pair),
                jnp.where(
                    lanes < 32,
                    roll_lanes(tile(q_ref, fr, pair + 1), 16 - 16 * pair),
                    roll_lanes(tile(v_ref, fr, pair + 1), 32 - 16 * pair),
                ),
            )
            joined = jnp.where(half_lanes < 64, left[0:half], roll_lanes(left[half:places], 64))
            sbk[fr, pair, places : places + half] = joined.astype(BF)

    def pack(ref, buf, fr):
        for pair in range(8):
            buf[fr, pair] = main_of(ref, fr, pair)

    sent = ((sbk, zrk, fk), (sbq, zrq, fq), (sbv, zrv, fv))

    def z_copy(t, j):
        buf, relay, final = sent[t]
        target = lax.rem(y + j, 8)
        return send(buf.at[far, target], relay.at[j], zs.at[t, j], zr.at[t, j], partner)

    def z_home(t):
        buf, relay, final = sent[t]
        return send(buf.at[far, y], final.at[s], zs.at[t, 0], zr.at[t, 0], partner)

    def y_copy(t, j):
        buf, relay, final = sent[t]
        target = lax.rem(y + j, 8)
        return send(
            buf.at[a, target], final.at[s], ys.at[0, t, j], yr.at[0, t, j], (f, a * 8 + target)
        )

    def y_relay(t, j):
        buf, relay, final = sent[t]
        target = lax.rem(y + j, 8)
        return send(
            relay.at[j], final.at[far * 8 + y], ys.at[1, t, j], yr.at[1, t, j],
            (f, a * 8 + target),
        )

    def each(low, high, body):
        def step(j, carry):
            body(j)
            return carry

        lax.fori_loop(low, high, step, 0)

    pack_k(far)
    pl.semaphore_wait(barrier, 20)

    def z_start(t):
        each(1, 8, lambda j: z_copy(t, j).start())
        z_home(t).start()

    def y_start(t):
        each(1, 8, lambda j: y_copy(t, j).start())

    z_start(0)
    pack(q_ref, sbq, far)
    z_start(1)
    pack(v_ref, sbv, far)
    z_start(2)
    pack_k(a)
    y_start(0)
    pack(q_ref, sbq, a)
    y_start(1)
    pack(v_ref, sbv, a)
    y_start(2)
    fk[s] = sbk[a, y]
    fq[s] = sbq[a, y]
    fv[s] = sbv[a, y]

    def forward(t, j):
        z_copy(t, j).wait_recv()
        y_relay(t, j).start()

    def settle(t):
        z_home(t).wait_recv()
        each(1, 8, lambda j: y_copy(t, j).wait_recv())
        each(1, 8, lambda j: y_relay(t, j).wait_recv())

    each(1, 8, lambda j: forward(0, j))
    each(1, 8, lambda j: forward(1, j))
    settle(0)

    zero = jnp.zeros((places, 128), F32)

    def spread(block):
        rows = pl.ds(pl.multiple_of(block * places, places), places)
        main = fk[block, 0:places].astype(F32)
        packed = fk[block, places : places + half].astype(F32)
        left = jnp.concatenate([packed, roll_lanes(packed, 64)], axis=0)
        k0[rows, :] = jnp.where(lanes < HEAD, main, zero).astype(BF)
        k1[rows, 0:128] = jnp.where(lanes < HEAD, zero, main).astype(BF)
        k1[rows, 128:256] = jnp.where(lanes < 16, left, zero).astype(BF)
        qs[rows, 128:256] = roll_lanes(left, -16).astype(BF)
        vs[rows, 128:256] = jnp.where(
            lanes < 16, roll_lanes(left, -32), jnp.where(lanes == 16, 1.0, 0.0)
        ).astype(BF)

    each(0, 16, spread)
    settle(1)

    def place_q(block):
        rows = pl.ds(pl.multiple_of(block * places, places), places)
        qs[rows, 0:128] = fq[block]

    each(0, 16, place_q)

    big = 4 * places

    def weigh(step):
        rows = pl.ds(pl.multiple_of(step * big, big), big)
        for head in range(2):
            if head == 0:
                left_side, keys = qs[rows, 0:128], k0[...]
            else:
                left_side, keys = qs[rows, :], k1[...]
            scores = lax.dot_general(
                left_side, keys, (((1,), (1,)), ((), ())), preferred_element_type=F32
            )
            largest = jnp.max(scores, axis=1, keepdims=True)
            pr[head, rows, :] = jnp.exp2((scores - largest) * EXP2_SCALE).astype(BF)
            if head == 0:
                forward(2, 2 * step + 1)

        @pl.when(step < 3)
        def _():
            forward(2, 2 * step + 2)

    each(0, 4, weigh)
    settle(2)

    def place_v(block):
        rows = pl.ds(pl.multiple_of(block * places, places), places)
        vs[rows, 0:128] = fv[block]

    each(0, 16, place_v)

    sub_lanes = lane_iota(16)

    def mix(first):
        rows = pl.ds(pl.multiple_of(first * places, places), big)
        mixed = []
        for head in range(2):
            product = jnp.dot(pr[head, rows, :], vs[...], preferred_element_type=F32)
            inverse = 1.0 / product[:, 144:145]
            mixed.append(product * inverse)
        for part in range(4):
            cut = slice(part * places, (part + 1) * places)
            ob[first + part, 0:places] = jnp.where(
                lanes < HEAD, mixed[0][cut, 0:128], mixed[1][cut, 0:128]
            ).astype(BF)
            rest = mixed[1][cut, 128:256]
            packed = rest[0:16]
            for group in range(1, 6):
                moved = roll_lanes(rest[16 * group : 16 * group + 16], 16 * group)
                packed = jnp.where(sub_lanes < 16 * group, packed, moved)
            ob[first + part, places : places + 16] = packed.astype(BF)

    def z_back(target):
        return send(
            ob.at[far * 8 + target], zro.at[target], zos.at[target], zor.at[target], partner
        )

    def z_back_home():
        return send(ob.at[far * 8 + y], mixb.at[1, y], zos.at[y], zor.at[y], partner)

    def y_back(j):
        target = lax.rem(y + j, 8)
        return send(
            ob.at[a * 8 + target], mixb.at[0, y], yos.at[0, j], yor.at[0, j],
            (f, a * 8 + target),
        )

    def y_back_relay(target):
        j = lax.rem(target + 8 - y, 8)
        return send(
            zro.at[target], mixb.at[1, y], yos.at[1, j], yor.at[1, j], (f, a * 8 + target)
        )

    def z_back_start(target):
        @pl.when(target != y)
        def _():
            z_back(target).start()

        @pl.when(target == y)
        def _():
            z_back_home().start()

    def far_part(step):
        mix(far * 8 + 4 * step)
        each(4 * step, 4 * step + 4, z_back_start)

    def near_part(step):
        mix(a * 8 + 4 * step)

    each(0, 2, far_part)
    each(0, 2, near_part)
    each(1, 8, lambda j: y_back(j).start())
    mixb[0, y] = ob[s]

    for load in loads[3:]:
        load.wait()

    def project(kind, frame):
        packs = [mixb[kind, pair, places : places + 16].astype(F32) for pair in range(8)]
        for pair in range(8):
            am[kind, :, 128 * pair : 128 * pair + 128] = mixb[kind, pair, 0:places]
        for group in range(6):
            joined = roll_lanes(packs[0], -16 * group)
            for pair in range(1, 8):
                moved = roll_lanes(packs[pair], 16 * pair - 16 * group)
                joined = jnp.where(sub_lanes < 16 * pair, joined, moved)
            am[kind, 16 * group : 16 * group + 16, 1024:1152] = joined.astype(BF)
        branch = jnp.dot(am[kind], wp[...], preferred_element_type=F32)
        res = (res_ref[frame].astype(F32) + mod_ref[2:3, :] * branch).astype(BF)
        res_out[frame] = res
        values = res.astype(F32)
        center = jnp.mean(values, axis=1, keepdims=True)
        moved = values - center
        deviation = jnp.mean(moved * moved, axis=1, keepdims=True)
        normed = moved * lax.rsqrt(deviation + 1e-06) * (1.0 + mod_ref[1:2, :]) + mod_ref[0:1, :]
        pf[0:places, 0:width] = lax.dot_general(
            normed.astype(BF), wt[...], (((1,), (1,)), ((), ())), preferred_element_type=F32
        )

        def cut(g):
            eight = pf[pl.ds(pl.multiple_of(8 * g, 8), 8), :]
            for t in range(4):
                sb[kind, 4 * g + t] = eight[2 * t : 2 * t + 2].astype(BF)

        each(0, places // 8, cut)

    def level_copy(kind, j):
        level = lax.rem(z + j, 6)
        return send(
            sb.at[kind, pl.ds(8 * level, 8)], zx.at[kind, z], ts.at[kind, level], tr.at[kind, z],
            peer(kme, level),
        )

    def level_arrival(kind, level):
        return send(
            sb.at[kind, pl.ds(0, 8)], zx.at[kind, level], ts.at[kind, level], tr.at[kind, level],
            peer(kme, level),
        )

    def row_copy(kind, level, j, own):
        k = lax.rem(kme + j, 8)
        source = sb.at[kind, 8 * z + k] if own else zx.at[kind, level, k]
        return send(
            source, rb.at[kind, level * 8 + kme], xs.at[kind, level, k], xr.at[kind, level, kme],
            peer(k, z),
        )

    def row_arrival(kind, level, j):
        k = lax.rem(kme + j, 8)
        return send(
            sb.at[kind, 0], rb.at[kind, level * 8 + k], xs.at[kind, level, k],
            xr.at[kind, level, k], peer(k, z),
        )

    def exchange(kind):
        for j in ORDER:
            level_copy(kind, j).start()
        each(1, 8, lambda j: row_copy(kind, z, j, True).start())
        rb[kind, 8 * z + kme] = sb[kind, 8 * z + kme]

    def relay_level(kind, j):
        level = lax.rem(z + j, 6)
        level_arrival(kind, level).wait_recv()
        each(1, 8, lambda i: row_copy(kind, level, i, False).start())
        rb[kind, 8 * level + kme] = zx[kind, level, kme]

    each(1, 8, lambda j: y_back(j).wait_recv())
    width = wt.shape[0]
    inner = width // 3
    pf[:, 1664:1792] = jnp.zeros((2 * places, 128), F32)
    project(0, a)
    exchange(0)
    def relay_back(target):
        @pl.when(target != y)
        def _():
            z_back(target).wait_recv()
            y_back_relay(target).start()

    each(0, 8, relay_back)
    z_back_home().wait_recv()

    def relay_end(j):
        copy = send(
            zro.at[0], mixb.at[1, 0], yos.at[1, j], yor.at[1, j], (f, a * 8 + lax.rem(y + j, 8))
        )
        copy.wait_recv()
        copy.wait_send()

    each(1, 8, relay_end)
    each(1, 8, lambda j: y_back(j).wait_send())

    project(1, far)
    exchange(1)
    for j in ORDER:
        relay_level(0, 6 - j)
    for kind in range(2):
        for j in ORDER:
            if kind == 1:
                relay_level(kind, 6 - j)

    def gather(kind, level):
        each(1, 8, lambda j: row_arrival(kind, level, j).wait_recv())
        for half_row in range(2):
            parts = [rb[kind, 8 * level + 4 * half_row + t].astype(F32) for t in range(4)]
            start = pl.multiple_of(kind * 96 + 16 * level + 8 * half_row, 8)
            pf[pl.ds(start, 8), :] = jnp.concatenate(parts, axis=0)

    for kind in range(2):
        for j in (0,) + ORDER:
            gather(kind, lax.rem(z + 6 - j, 6))

    by_place = one_hot(
        lambda r: (lax.rem(r, 96) // 48) * 96 + 2 * lax.rem(r, 48) + r // 96
    )
    to_group = one_hot(
        lambda r: lax.rem(r, 2) * 96 + lax.rem(r // 2, 2) * 48 + r // 4
    )
    to_rows = one_hot(
        lambda r: 4 * (lax.rem(r, 96) // 2) + 2 * (r // 96) + lax.rem(r, 2)
    )
    rows = jnp.dot(by_place, pf[...].astype(BF), preferred_element_type=F32).astype(BF)
    lanes256 = lax.broadcasted_iota(jnp.int32, (96, 256), 1)
    tm[...] = jnp.zeros(tm.shape, F32)
    for p in range(2):
        block = rows[p * 96 : p * 96 + 96]
        for head in range(T_HEADS):
            start = head * HEAD
            queries = block[:, start : start + HEAD]
            keys = block[:, inner + start : inner + start + HEAD]
            window = min((start // 128) * 128, 384)
            scores = lax.dot_general(
                queries, keys, (((1,), (1,)), ((), ())), preferred_element_type=F32
            )
            largest = jnp.max(scores, axis=1, keepdims=True)
            expons = jnp.exp2((scores - largest) * EXP2_SCALE)
            totals = jnp.sum(expons, axis=1, keepdims=True)
            vals = block[:, 2 * inner + window : min(2 * inner + window + 256, 1792)]
            product = jnp.dot(expons.astype(BF), vals, preferred_element_type=F32) / totals
            near = lanes256[:, : vals.shape[1]] + window
            held = (near >= start) & (near < start + HEAD)
            spot = (slice(p * 96, p * 96 + 96), slice(window, window + vals.shape[1]))
            tm[spot] = jnp.where(held, product, tm[spot])

    pf[:, 0:640] = jnp.dot(to_group, tm[...].astype(BF), preferred_element_type=F32)

    def cut_back(g):
        both = pf[pl.ds(pl.multiple_of(8 * g, 8), 8), 0:640]
        sb2[2 * g] = both[0:4].astype(BF)
        sb2[2 * g + 1] = both[4:8].astype(BF)

    each(0, 24, cut_back)

    def level_home(j):
        level = lax.rem(z + j, 6)
        return send(
            sb2.at[pl.ds(8 * level, 8)], zx2.at[z], us.at[level], ur.at[z], peer(kme, level)
        )

    def level_home_arrival(level):
        return send(
            sb2.at[pl.ds(0, 8)], zx2.at[level], us.at[level], ur.at[level], peer(kme, level)
        )

    def row_home(level, j, own):
        k = lax.rem(kme + j, 8)
        source = sb2.at[8 * z + k] if own else zx2.at[level, k]
        return send(
            source, rb2.at[level * 8 + kme], ws.at[level, k], wr.at[level, kme], peer(k, z)
        )

    def row_home_arrival(level, j):
        k = lax.rem(kme + j, 8)
        return send(
            sb2.at[0], rb2.at[level * 8 + k], ws.at[level, k], wr.at[level, k], peer(k, z)
        )

    for j in ORDER:
        level_home(j).start()
    each(1, 8, lambda j: row_home(z, j, True).start())
    rb2[8 * z + kme] = sb2[8 * z + kme]
    for j in ORDER:
        level = lax.rem(z + 6 - j, 6)
        level_home_arrival(level).wait_recv()
        each(1, 8, lambda i: row_home(level, i, False).start())
        rb2[8 * level + kme] = zx2[level, kme]

    def gather_back(level):
        each(1, 8, lambda j: row_home_arrival(level, j).wait_recv())
        for part in range(4):
            start = pl.multiple_of(32 * level + 8 * part, 8)
            pair = 8 * level + 2 * part
            pf[pl.ds(start, 8), 0:640] = jnp.concatenate(
                [rb2[pair].astype(F32), rb2[pair + 1].astype(F32)], axis=0
            )

    for j in (0,) + ORDER:
        gather_back(lax.rem(z + 6 - j, 6))
    final = jnp.dot(to_rows, pf[:, 0:640].astype(BF), preferred_element_type=F32)
    mix_out[a] = final[0:96, 0:inner].astype(BF)
    mix_out[far] = final[96:192, 0:inner].astype(BF)

    for j in ORDER:
        for kind in range(2):
            level_copy(kind, j).wait_send()
        level_home(j).wait_send()

    def drain(level):
        def one(j):
            for kind in range(2):
                row_copy(kind, level, j, False).wait_send()
            row_home(level, j, False).wait_send()

        each(1, 8, one)

    each(0, 6, drain)
    each(0, 8, lambda target: z_back(target).wait_send())
    for t in range(3):
        z_home(t).wait_send()
        each(1, 8, lambda j: z_copy(t, j).wait_send())
        each(1, 8, lambda j: y_copy(t, j).wait_send())
        each(1, 8, lambda j: y_relay(t, j).wait_send())


def per_device(residual_in, q_spatial, k_spatial, v_spatial, w_out, modulation, w_temporal):
    frames, places, features = residual_in.shape
    half = places // 2
    total = 16 * places
    width = w_temporal.shape[1]
    vmem = pl.BlockSpec(memory_space=pltpu.VMEM)
    hbm = pl.BlockSpec(memory_space=pl.ANY)
    dma = pltpu.SemaphoreType.DMA
    local = (frames, places, features)
    return pl.pallas_call(
        block_kernel,
        out_shape=(
            jax.ShapeDtypeStruct(local, BF),
            jax.ShapeDtypeStruct((frames, places, width // 3), BF),
        ),
        in_specs=[hbm] * 5 + [vmem, hbm],
        out_specs=(vmem, vmem),
        scratch_shapes=[
            pltpu.VMEM(local, BF),
            pltpu.VMEM(local, BF),
            pltpu.VMEM(local, BF),
            pltpu.VMEM(local, BF),
            pltpu.VMEM((features, features), BF),
            pltpu.VMEM((width, features), BF),
            pltpu.VMEM((2, 8, places + half, 128), BF),
            pltpu.VMEM((2, 8, places, 128), BF),
            pltpu.VMEM((2, 8, places, 128), BF),
            pltpu.VMEM((8, places + half, 128), BF),
            pltpu.VMEM((8, places, 128), BF),
            pltpu.VMEM((8, places, 128), BF),
            pltpu.VMEM((16, places + half, 128), BF),
            pltpu.VMEM((16, places, 128), BF),
            pltpu.VMEM((16, places, 128), BF),
            pltpu.VMEM((total, 256), BF),
            pltpu.VMEM((total, 128), BF),
            pltpu.VMEM((total, 256), BF),
            pltpu.VMEM((total, 256), BF),
            pltpu.VMEM((2, total, total), BF),
            pltpu.VMEM((16, places + 16, 128), BF),
            pltpu.VMEM((8, places + 16, 128), BF),
            pltpu.VMEM((2, 8, places + 16, 128), BF),
            pltpu.VMEM((2, places, features), BF),
            pltpu.VMEM((2 * places, 1792), F32),
            pltpu.VMEM((2, 48, 2, 1792), BF),
            pltpu.VMEM((2, 6, 8, 2, 1792), BF),
            pltpu.VMEM((2, 48, 2, 1792), BF),
            pltpu.VMEM((2 * places, 640), F32),
            pltpu.VMEM((48, 4, 640), BF),
            pltpu.VMEM((6, 8, 4, 640), BF),
            pltpu.VMEM((48, 4, 640), BF),
            dma((21,)),
            dma((3, 8)), dma((3, 8)), dma((2, 3, 8)), dma((2, 3, 8)),
            dma((8,)), dma((8,)), dma((2, 8)), dma((2, 8)),
            dma((2, 6)), dma((2, 6)), dma((2, 6, 8)), dma((2, 6, 8)),
            dma((6,)), dma((6,)), dma((6, 8)), dma((6, 8)),
        ],
        compiler_params=pltpu.CompilerParams(
            collective_id=1, has_side_effects=True, vmem_limit_bytes=67043328
        ),
        name="block",
    )(residual_in, q_spatial, k_spatial, v_spatial, w_out, modulation, w_temporal.T)


def solution(mesh):
    return jax.shard_map(
        per_device,
        mesh=mesh,
        in_specs=(
            P("frame", "space", None),
            P("frame", "space", None),
            P("frame", "space", None),
            P("frame", "space", None),
            P(),
            P(),
            P(),
        ),
        out_specs=(P("frame", "space", None), P("frame", "space", None)),
        check_vma=False,
    )
```
